128 devices in a mesh: face: 8 (over y_lo, x), tile: 16 (over y_hi, z, core).
Axes of the slice: x: 4, y: 4 (y_hi: 2, y_lo: 2; y = y_hi * 2 + y_lo), z: 4, core: 2. Of those that a mesh axis runs over, the one named last changes fastest.
Arguments:
- atmos_state: bfloat16 [128, 1024, 2048], P(None, 'face', 'tile'), may hold values from -6 to 6
- ocean_state: bfloat16 [64, 1024, 2048], P(None, 'face', 'tile'), may hold values from -6 to 6
- land_mask: int32 [1024, 64], P('face', 'tile'), may hold values 0 or 1
- face_turns: int32 [8, 16], P('face', 'tile'), may hold values from 0 to 3
- block_target: int32 [16384, 1], P(('face', 'tile')), may hold values from 0 to 127; in each aligned block of 128 rows (0 to 127, 128 to 255, ...) at most 2 rows name the same one
- block_patch: int32 [16384, 1], P(('face', 'tile')), may hold values from 0 to 127
- block_weight: float32 [16384, 1], P(('face', 'tile')), may hold values from 0.25 to 1
- atmos_w1: bfloat16 [9, 128, 144], replicated, may hold values from -0.15625 to 0.15625
- atmos_w2: bfloat16 [9, 128, 128], replicated, may hold values from -0.1875 to 0.1875
- ocean_w1: bfloat16 [9, 64, 80], replicated, may hold values from -0.21875 to 0.21875
- ocean_w2: bfloat16 [9, 64, 64], replicated, may hold values from -0.25 to 0.25
Outputs:
- atmos_out: bfloat16 [128, 1024, 2048], P(None, 'face', 'tile')
- ocean_out: bfloat16 [64, 1024, 2048], P(None, 'face', 'tile')
The draws below stay inside these ranges and needn't reach their ends.
Inputs may be any that keep to these rules, and one draw needn't show every extreme that they name: `block_target`: among the 128 blocks of one device, at most 2 have the same target, and in every draw some device has exactly 2 blocks with one target.
All inputs are finite; a program needn't handle non-finite values. No bound on the sum of `land_mask` on one device may be relied on, other than what follows from the above.
Results may differ from the reference program's by a relative error of at most 0.001.
The reference program's roundings to bfloat16 on the way (of `common`, `masked_ocean`, `weights`, `sea_surface`, `forcing`, `hidden_atmos`, `atmos_common_out` and `hidden_ocean`) count: a program that leaves them out, or rounds other values in their place, can miss the bound.
Values may be sent and summed in bfloat16 or wider, within the bound.
A program may use at most 192 MiB of HBM per device.

```python
import math
from functools import partial
import jax
import jax.numpy as jnp
import numpy as np
from jax import lax

CA = 128
CO = 64
CS = 16
CF = 16
S = 128
OH = 128
NAY = 1024
NAX = 2048
NOY = 1024
NOX = 2048
BLOCKS = 16384
CAP = 2
N_FACE = 8
N_TILE = 16
DEVICES = 128


def set_ends(values, rng, low, largest):
    shape = values.shape
    index_at = [jax.random.randint(jax.random.fold_in(rng, axis), (), 0, shape[axis]) for axis in range(len(shape))]
    values = values.at[tuple(index_at)].set(low)
    longest = shape.index(max(shape))
    index_at[longest] = (index_at[longest] + 1) % shape[longest]
    return values.at[tuple(index_at)].set(largest)


def levels(key, shape, split, least, top_value):
    loudness = 1.0
    for axis_at, blocks in split:
        steps = jax.random.uniform(jax.random.fold_in(jax.random.fold_in(key, 6), axis_at), (blocks,), jnp.float32, least / len(split), top_value / len(split))
        loudness = loudness * jnp.repeat(jnp.exp(steps), shape[axis_at] // blocks).reshape((-1,) + (1,) * (len(shape) - 1 - axis_at))
    return loudness


def assign_block(own_key, own, number, rows, number_of, top, most, slope):
    order = jax.random.permutation(own_key, number_of)
    heavy_load, usual = load_shares(number_of, rows * top, most, slope, True), load_shares(number_of, rows * top, most, slope, False)
    places = jnp.arange(number_of)

    def named(tallies, turn):
        used = int((tallies > 0).sum())
        fixed = max(1, used // 4)
        moved = fixed + (places - fixed + turn * (used - fixed)) % max(1, number_of - fixed)
        return jnp.zeros((number_of,), jnp.int32).at[order[jnp.where(places < fixed, places, moved)]].set(jnp.asarray(tallies, jnp.int32))

    tallies = jnp.where(number % 4 == 0, named(heavy_load, number // 4), named(usual, number - number // 4 - 1))
    mixed = jax.random.permutation(jax.random.fold_in(own, 3), number_of)
    donor, taker = mixed[0:number_of // 2 * 2:2], mixed[1:number_of // 2 * 2:2]
    room = jnp.minimum(tallies[donor] - 1, most - tallies[taker]) // 2
    room = jnp.where((donor == order[0]) | (taker == order[0]) | (tallies[taker] == 0), 0, jnp.maximum(room, 0))
    moved = jax.random.randint(jax.random.fold_in(own, 4), (number_of // 2,), 0, 1 << 20) % (room + 1)
    tallies = tallies.at[donor].add(-moved).at[taker].add(moved)
    labels = jnp.searchsorted(jnp.cumsum(tallies), jnp.arange(rows * top), side="right").astype(jnp.int32)
    grid = labels.reshape(top, rows).T
    grid = grid[jax.random.permutation(jax.random.fold_in(own, 1), rows)]
    turn = jax.random.randint(jax.random.fold_in(own, 2), (rows, 1), 0, top)
    return jnp.take_along_axis(grid, (jnp.arange(top)[None, :] + turn) % top, axis=1)


def load_shares(amount, total, most, slope, full):
    loads = [(1 << 20) // math.isqrt(rank ** slope) + 1 for rank in range(1, amount + 1)]
    largest = most if full else min(most, max(-(-total // amount), total * loads[0] // sum(loads)))
    least = 1 if total - largest >= amount - 1 else 0
    counts, surplus = [largest] + [least] * (amount - 1), total - largest - least * (amount - 1)
    while surplus > 0:
        movable = [i for i in range(1, amount) if counts[i] < largest] or [i for i in range(1, amount) if counts[i] < most]
        whole, budget = sum([loads[i] for i in movable]), surplus
        for i in movable:
            extra = min(most - counts[i], max(1, budget * loads[i] // whole), surplus)
            counts[i] = counts[i] + extra
            surplus = surplus - extra
    return np.array(counts)


def scatter_about(rng, shape, spread, reach, pieces=(), held_as=jnp.bfloat16):
    values = spread * jax.random.normal(rng, shape, jnp.float32)
    if pieces:
        values = values * levels(rng, shape, pieces, -0.22, 0.18)
    return jnp.clip(values, -reach, reach).astype(held_as)


def setup_inputs(seed: int = 0) -> dict:
    key_list = jax.random.split(jax.random.key(seed), 12)
    atmos_state = scatter_about(key_list[0], (CA, NAY, NAX), 1.0, 6.0, ((1, 8), (2, 16)))
    ocean_state = scatter_about(key_list[1], (CO, NOY, NOX), 1.0, 6.0, ((1, 8), (2, 16)))
    land_mask = set_ends((jax.random.randint(key_list[2], (NOY, NOX // 32), 0, 4) < 3).astype(jnp.int32), jax.random.fold_in(key_list[2], 1), 0, 1)
    face_turns = set_ends(jax.random.randint(key_list[3], (N_FACE, N_TILE), 0, 4), jax.random.fold_in(key_list[3], 1), 0, 3).astype(jnp.int32)
    block_target_keys = jax.random.split(jax.random.fold_in(key_list[4], 1), BLOCKS // OH)
    block_target_turns = jax.random.permutation(jax.random.fold_in(key_list[4], 3), BLOCKS // OH)
    block_target = jax.vmap(lambda own, number: assign_block(jax.random.fold_in(key_list[4], 2), own, number, OH, DEVICES, 1, CAP, 2))(block_target_keys, block_target_turns).reshape((BLOCKS, 1))
    block_patch = set_ends(jax.random.randint(key_list[5], (BLOCKS, 1), 0, S), jax.random.fold_in(key_list[5], 1), 0, S - 1).astype(jnp.int32)
    block_weight = jnp.clip(jnp.exp(math.log(1.0) - 1.3862944 * jax.random.uniform(key_list[6], (BLOCKS, 1), jnp.float32) ** levels(key_list[6], (BLOCKS, 1), ((0, 128),), -0.2, 0.2)), 0.25, 1.0)
    atmos_w1 = scatter_about(key_list[7], (9, CA, CA + CS), (9 * (CA + CS)) ** -0.5, 0.15625)
    atmos_w2 = scatter_about(key_list[8], (9, CA, CA), (9 * CA) ** -0.5, 0.1875)
    ocean_w1 = scatter_about(key_list[9], (9, CO, CO + CF), (9 * (CO + CF)) ** -0.5, 0.21875)
    ocean_w2 = scatter_about(key_list[10], (9, CO, CO), (9 * CO) ** -0.5, 0.25)
    return {"atmos_state": atmos_state, "ocean_state": ocean_state, "land_mask": land_mask, "face_turns": face_turns, "block_target": block_target, "block_patch": block_patch, "block_weight": block_weight, "atmos_w1": atmos_w1, "atmos_w2": atmos_w2, "ocean_w1": ocean_w1, "ocean_w2": ocean_w2}


def turn_tile(tile_data, quarter_turns):
    return jnp.rot90(tile_data, quarter_turns, axes=(1, 2))


def turn_all(tiles, turns, sign):
    branches = [partial(turn_tile, quarter_turns=sign * quarter) for quarter in range(4)]

    def apply_turn(packed):
        return lax.switch(packed[1], branches, packed[0])

    return lax.map(apply_turn, (tiles, turns))


def to_tiles(values):
    channels = values.shape[0]
    shaped = values.reshape(channels, N_FACE, S, N_TILE, S).transpose(1, 3, 0, 2, 4)
    return shaped.reshape(N_FACE * N_TILE, channels, S, S)


def from_tiles(tiles):
    channels = tiles.shape[1]
    shaped = tiles.reshape(N_FACE, N_TILE, channels, S, S).transpose(2, 0, 3, 1, 4)
    return shaped.reshape(channels, N_FACE * S, N_TILE * S)


def convolve(padded, weight, block_rows, finish):
    col_count = padded.shape[2] - 2
    block_count = (padded.shape[1] - 2) // block_rows
    kernel = weight.astype(jnp.float32)

    def one_block(block_id):
        part = lax.dynamic_slice_in_dim(padded, block_id * block_rows, block_rows + 2, 1).astype(jnp.float32)
        summed = jnp.zeros((kernel.shape[1], block_rows, col_count), jnp.float32)
        for row_shift in range(3):
            for col_shift in range(3):
                window = part[:, row_shift:row_shift + block_rows, col_shift:col_shift + col_count]
                summed = summed + jnp.einsum("oc,cyx->oyx", kernel[row_shift * 3 + col_shift], window)
        return finish(summed, block_id)

    result = lax.map(one_block, jnp.arange(block_count, dtype=jnp.int32))
    return result.transpose(1, 0, 2, 3).reshape(result.shape[1], block_count * block_rows, col_count)


def wrap_pad(values):
    return jnp.pad(values, ((0, 0), (1, 1), (1, 1)), mode="wrap")


def fold_pad(values):
    wrapped = jnp.pad(values, ((0, 0), (0, 0), (1, 1)), mode="wrap")
    north_row = wrapped[:, -1:, ::-1]
    south_row = jnp.zeros_like(north_row)
    return jnp.concatenate([south_row, wrapped, north_row], axis=1)


def activate(summed, block_id):
    return jax.nn.gelu(summed, approximate=True).astype(jnp.bfloat16)


def reference(atmos_state, ocean_state, land_mask, face_turns, block_target, block_patch, block_weight, atmos_w1, atmos_w2, ocean_w1, ocean_w2):
    tile_total = N_FACE * N_TILE
    turns = face_turns.reshape(-1)
    common = from_tiles(turn_all(to_tiles(atmos_state), turns, -1))
    mask_cells = jnp.repeat(land_mask, 32, axis=1).astype(jnp.bfloat16)
    masked_ocean = ocean_state * mask_cells[None]
    ocean_blocks = masked_ocean[:CS].reshape(CS, N_FACE, OH, N_TILE, S).transpose(1, 3, 2, 0, 4)
    ocean_blocks = ocean_blocks.reshape(tile_total * OH, CS * S).astype(jnp.float32)
    rounded = lax.optimization_barrier(block_weight[:, 0].astype(jnp.bfloat16))
    weights = rounded.astype(jnp.float32)
    patch_ids = (block_target[:, 0] * S + block_patch[:, 0]).astype(jnp.int32)
    numerator = jax.ops.segment_sum(ocean_blocks * weights[:, None], patch_ids, num_segments=tile_total * S)
    denominator = jax.ops.segment_sum(weights, patch_ids, num_segments=tile_total * S)
    sea_rows = (numerator / jnp.maximum(denominator, 1.0)[:, None]).astype(jnp.bfloat16)
    sea_surface = sea_rows.reshape(N_FACE, N_TILE, S, CS, S).transpose(3, 0, 2, 1, 4).reshape(CS, N_FACE * S, N_TILE * S)
    atmos_rows = common[:CF].reshape(CF, N_FACE, S, N_TILE, S).transpose(1, 3, 2, 0, 4).reshape(tile_total * S, CF * S)
    facing = jnp.take(atmos_rows, patch_ids, axis=0)
    forcing = facing.reshape(N_FACE, N_TILE, OH, CF, S).transpose(3, 0, 2, 1, 4).reshape(CF, N_FACE * OH, N_TILE * S)

    atmos_in = jnp.concatenate([common, sea_surface], axis=0)
    hidden_atmos = convolve(wrap_pad(atmos_in), atmos_w1, S, activate)

    def finish_atmos(summed, block_id):
        base = lax.dynamic_slice_in_dim(common, block_id * S, S, 1).astype(jnp.float32)
        return (base + summed).astype(jnp.bfloat16)

    atmos_common_out = convolve(wrap_pad(hidden_atmos), atmos_w2, S, finish_atmos)
    atmos_out = from_tiles(turn_all(to_tiles(atmos_common_out), turns, 1))

    ocean_in = jnp.concatenate([masked_ocean, forcing], axis=0)
    hidden_ocean = convolve(fold_pad(ocean_in), ocean_w1, OH, activate)
    mask_float = mask_cells.astype(jnp.float32)

    def finish_ocean(summed, block_id):
        base = lax.dynamic_slice_in_dim(masked_ocean, block_id * OH, OH, 1).astype(jnp.float32)
        gate = lax.dynamic_slice_in_dim(mask_float, block_id * OH, OH, 0)
        return (gate[None] * (base + summed)).astype(jnp.bfloat16)

    ocean_out = convolve(fold_pad(hidden_ocean), ocean_w2, OH, finish_ocean)
    return atmos_out, ocean_out
```

```python
from functools import partial

import jax
import jax.numpy as jnp
from jax import lax
from jax.experimental import pallas as pl
from jax.experimental.pallas import tpu as pltpu
from jax.sharding import PartitionSpec as P

BF = jnp.bfloat16
F32 = jnp.float32
S = 128
CS = 16
MESH = pl.DeviceIdType.MESH
VMEM = pltpu.VMEM
SMEM = pltpu.SMEM

UP, DOWN, LEFT, RIGHT, UL, UR, DL, DR = range(8)
TO_STORED = (
    ((UP, 0), (RIGHT, 0), (DOWN, 1), (LEFT, 1)),
    ((DOWN, 0), (LEFT, 0), (UP, 1), (RIGHT, 1)),
    ((LEFT, 0), (UP, 1), (RIGHT, 1), (DOWN, 0)),
    ((RIGHT, 0), (DOWN, 1), (LEFT, 1), (UP, 0)),
    ((UL, 0), (UR, 1), (DR, 1), (DL, 0)),
    ((UR, 0), (DR, 0), (DL, 1), (UL, 1)),
    ((DL, 0), (UL, 0), (UR, 1), (DR, 1)),
    ((DR, 0), (DL, 1), (UL, 1), (UR, 0)),
)
TO_COMMON = (
    ((UP, 0), (LEFT, 1), (DOWN, 1), (RIGHT, 0)),
    ((DOWN, 0), (RIGHT, 1), (UP, 1), (LEFT, 0)),
    ((LEFT, 0), (DOWN, 0), (RIGHT, 1), (UP, 1)),
    ((RIGHT, 0), (UP, 0), (LEFT, 1), (DOWN, 1)),
)


def anti():
    rows = lax.broadcasted_iota(jnp.int32, (S, S), 0)
    cols = lax.broadcasted_iota(jnp.int32, (S, S), 1)
    return jnp.where(rows + cols == S - 1, 1.0, 0.0).astype(BF)


def eye():
    rows = lax.broadcasted_iota(jnp.int32, (S, S), 0)
    cols = lax.broadcasted_iota(jnp.int32, (S, S), 1)
    return jnp.where(rows == cols, 1.0, 0.0).astype(BF)


def dot(a, b):
    return jnp.dot(a, b, preferred_element_type=F32)


def dot_nt(a, b):
    return lax.dot_general(a, b, (((1,), (1,)), ((), ())), preferred_element_type=F32)


def roll(v, shift):
    return pltpu.roll(v, shift % S, 1)


def lanes(channels):
    return lax.broadcasted_iota(jnp.int32, (channels, S), 1)


def reversed_lanes(v):
    return dot(v, anti()).astype(BF)


def select_sides(table, mode, source, target):
    for turn in range(4):

        @pl.when(mode == turn)
        def _():
            for i, row in enumerate(table):
                side, flip = row[turn]
                v = source[side]
                target[i] = reversed_lanes(v) if flip else v


def ocean_sides(mode, source, target):
    for i in range(8):
        target[i] = source[i]

    @pl.when(mode == 1)
    def _():
        for i in (UP, UL, UR):
            target[i] = jnp.zeros_like(target[i])

    @pl.when(mode == 2)
    def _():
        for i in (DOWN, DL, DR):
            target[i] = reversed_lanes(source[i])


def turn_matrix(v, turns):
    if turns == 1:
        return dot_nt(anti(), v)
    if turns == 2:
        return dot(dot(anti(), v).astype(BF), anti())
    if turns == 3:
        return dot_nt(eye(), dot(anti(), v).astype(BF))
    return v.astype(F32)


def conv_rows(parts, sides, runs, w_ref, outs, carry, finish, flush, unroll):
    first = [lanes(p.shape[1]) == 0 for p in parts]
    last = [lanes(p.shape[1]) == S - 1 for p in parts]
    for side, run in zip(sides, runs):
        run[0] = side[LEFT]
        run[1] = roll(side[LEFT], 64)
        run[2] = roll(side[RIGHT], 1)
        run[3] = roll(side[RIGHT], 65)

    def products(r, first_row, end):
        left, centre, right = [], [], []
        for n, (p, side, run) in enumerate(zip(parts, sides, runs)):
            la, lb, ra, rb = run[0], run[1], run[2], run[3]
            run[0], run[1], run[2], run[3] = roll(la, -1), roll(lb, -1), roll(ra, -1), roll(rb, -1)
            if first_row:
                xa, la, ra = side[UP], side[UL], side[UR]
            else:
                xa = p[r - 1]
            if end is None:
                xb = p[r + 63]
            else:
                xb = jnp.where(end, side[DOWN], p[jnp.minimum(r + 63, S - 1)])
                lb, rb = jnp.where(end, side[DL], lb), jnp.where(end, side[DR], rb)
            both = lambda a, b: jnp.concatenate([a, b], axis=1)
            left.append(both(roll(jnp.where(last[n], la, xa), 1), roll(jnp.where(last[n], lb, xb), 1)))
            centre.append(both(xa, xb))
            right.append(both(roll(jnp.where(first[n], ra, xa), -1), roll(jnp.where(first[n], rb, xb), -1)))
        return dot(w_ref[...], jnp.concatenate(left + centre + right, axis=0))

    o = outs
    p0 = products(0, True, None)
    p1 = products(1, False, None)
    carry[0] = p0[:o] + p1[o : 2 * o]
    carry[1] = p1[:o]

    def sixteen(g, _):
        def body(i, _):
            done, near = carry[0], carry[1]
            for u in range(unroll):
                y = g * 16 + i * unroll + u
                p = products(y + 2, False, y == 63 if u == unroll - 1 else None)
                finish(y, done + p[2 * o :])
                done, near = near + p[o : 2 * o], p[:o]
            carry[0], carry[1] = done, near
            return 0

        lax.fori_loop(0, 16 // unroll, body, 0)
        if flush is not None:
            flush(g)
        return 0

    lax.fori_loop(0, 4, sixteen, 0)


def hidden_kernel(ocean, unroll, count, mode_ref, *refs):
    parts, refs = refs[:count], refs[count:]
    halos, refs = refs[:count], refs[count:]
    w_ref, hid_ref, edge_ref, refs = refs[0], refs[1], refs[2], refs[3:]
    sides, refs = refs[:count], refs[count:]
    runs, refs = refs[:count], refs[count:]
    carry, cols, own = refs
    mode = mode_ref[0]
    for halo, side in zip(halos, sides):
        if ocean:
            ocean_sides(mode, halo, side)
        else:
            select_sides(TO_STORED, mode, halo, side)
    outs = hid_ref.shape[1]
    first, last = lanes(outs) == 0, lanes(outs) == S - 1

    def finish(y, both):
        for half in range(2):
            v = jax.nn.gelu(both[:, half * S : (half + 1) * S], approximate=True).astype(BF)
            hid_ref[y + 64 * half] = v
            cols[half] = roll(jnp.where(first, v, cols[half]), -1)
            cols[2 + half] = jnp.where(last, v, roll(cols[2 + half], -1))

    conv_rows(parts, sides, runs, w_ref, outs, carry, finish, None, unroll)
    upper = lanes(outs) >= 64
    own[UP], own[DOWN] = hid_ref[0], hid_ref[S - 1]
    own[LEFT] = jnp.where(upper, cols[1], roll(cols[0], 64))
    own[RIGHT] = jnp.where(upper, cols[3], roll(cols[2], 64))
    if ocean:
        for i in range(4):
            edge_ref[i] = own[i]
    else:
        select_sides(TO_COMMON, mode, own, edge_ref)


def hidden_conv(ocean, mode, parts, halos, weight, unroll):
    outs = weight.shape[0] // 3
    count = len(parts)
    channels = [p.shape[1] for p in parts]
    vm = pl.BlockSpec(memory_space=VMEM)
    return pl.pallas_call(
        partial(hidden_kernel, ocean, unroll, count),
        out_shape=(
            jax.ShapeDtypeStruct((S, outs, S), BF),
            jax.ShapeDtypeStruct((4, outs, S), BF),
        ),
        in_specs=[pl.BlockSpec(memory_space=SMEM)] + [vm] * (2 * count + 1),
        out_specs=(vm, vm),
        scratch_shapes=[VMEM((8, c, S), BF) for c in channels]
        + [VMEM((4, c, S), BF) for c in channels]
        + [VMEM((2, outs, 2 * S), F32), VMEM((4, outs, S), BF), VMEM((4, outs, S), BF)],
        name="hidden_ocean" if ocean else "hidden_atmos",
    )(mode, *parts, *halos, weight)


def out_kernel(ocean, unroll, mode_ref, hid_ref, halo_ref, w_ref, base_ref, mask_ref, out_ref, side, run, carry, stage):
    mode = mode_ref[0]
    if ocean:
        ocean_sides(mode, halo_ref, side)
    else:
        select_sides(TO_STORED, mode, halo_ref, side)
    outs = hid_ref.shape[1]

    def finish(y, both):
        place = lax.rem(y, 16)
        for half in range(2):
            stage[half, pl.ds(place, outs, stride=16), :] = both[:, half * S : (half + 1) * S]

    def flush(g):
        for half in range(2):
            rows = pl.ds(pl.multiple_of(g * 16 + 64 * half, 16), 16)
            base = base_ref[:, rows, :].astype(F32)
            summed = stage[half].reshape(outs, 16, S)
            if ocean:
                gate = mask_ref[rows, :].astype(F32)[None]
                out_ref[:, rows, :] = (gate * (gate * base + summed)).astype(BF)
            else:
                out_ref[:, rows, :] = (base + summed).astype(BF)

    conv_rows([hid_ref], [side], [run], w_ref, outs, carry, finish, flush, unroll)


def out_conv(ocean, mode, hidden, halo, weight, base, mask, unroll):
    outs = hidden.shape[1]
    vm = pl.BlockSpec(memory_space=VMEM)
    return pl.pallas_call(
        partial(out_kernel, ocean, unroll),
        out_shape=jax.ShapeDtypeStruct((outs, S, S), BF),
        in_specs=[pl.BlockSpec(memory_space=SMEM)] + [vm] * 5,
        out_specs=vm,
        scratch_shapes=[
            VMEM((8, outs, S), BF),
            VMEM((4, outs, S), BF),
            VMEM((2, outs, 2 * S), F32),
            VMEM((2, outs * 16, S), F32),
        ],
        name="out_ocean" if ocean else "out_atmos",
    )(mode, hidden, halo, weight, base, mask)


def prep_kernel(
    turn_ref, target_ref, patch_ref, weight_ref, atmos_ref, surface_ref, ocean_ref, mask_ref,
    xa_ref, xo_ref, ea_ref, eo_ref, pay_ref, meta_ref, common_ref, slot_ref,
    wide_a, wide_o, wide_s, cols_a, cols_o, own, surf, tally, patch_of, weight_of,
):
    step = pl.program_id(0)
    turn = turn_ref[0]

    def columns(cols, v):
        first, last = lanes(v.shape[0]) == 0, lanes(v.shape[0]) == S - 1
        cols[0] = roll(jnp.where(first, v, cols[0]), -1)
        cols[1] = jnp.where(last, v, roll(cols[1], -1))

    @pl.when(step == 0)
    def _():
        pay_ref[...] = jnp.zeros_like(pay_ref)

        def clear(p, _):
            tally[p] = 0
            for n in range(2):
                patch_of[2 * p + n] = 0
                weight_of[2 * p + n] = 0.0
            return 0

        lax.fori_loop(0, S, clear, 0)

    wide_a[...] = atmos_ref[...].astype(F32).reshape(wide_a.shape)
    gate = mask_ref[...].astype(F32)[None]
    wide_o[...] = (ocean_ref[...].astype(F32) * gate).reshape(wide_o.shape)
    for y in range(16):
        v = wide_a[pl.ds(y, S, stride=16), :].astype(BF)
        xa_ref[y] = v
        columns(cols_a, v)
        v = wide_o[pl.ds(y, eo_ref.shape[1], stride=16), :].astype(BF)
        xo_ref[y] = v
        columns(cols_o, v)
        surf[step * 16 + y] = v[:CS]

    @pl.when(step == 0)
    def _():
        own[UP] = xa_ref[0]
        eo_ref[UP] = xo_ref[0]

    @pl.when(step == 7)
    def _():
        own[DOWN], own[LEFT], own[RIGHT] = xa_ref[15], cols_a[0], cols_a[1]
        eo_ref[DOWN], eo_ref[LEFT], eo_ref[RIGHT] = xo_ref[15], cols_o[0], cols_o[1]
        select_sides(TO_COMMON, turn, own, ea_ref)

        def place(b, _):
            goal = target_ref[b]
            seen = tally[goal]
            slot = 2 * goal + seen
            tally[goal] = seen + 1
            slot_ref[b] = slot
            pay_ref[slot] = surf[b]
            patch_of[slot] = patch_ref[b]
            weight_of[slot] = weight_ref[b]
            return 0

        lax.fori_loop(0, S, place, 0)
        lane = lanes(1)

        def describe(p, _):
            places = jnp.where(lane == 0, patch_of[2 * p], patch_of[2 * p + 1]).astype(F32)
            shares = jnp.where(lane == 2, weight_of[2 * p], weight_of[2 * p + 1])
            meta_ref[p] = jnp.where(lane < 2, places, shares)
            return 0

        lax.fori_loop(0, S, describe, 0)
        for quarter in range(4):

            @pl.when(turn == quarter)
            def _():
                for c in range(CS):
                    wide_s[pl.ds(c, S, stride=CS), :] = turn_matrix(surface_ref[c], (4 - quarter) % 4)

        common_ref[...] = wide_s[...].reshape(S, CS, S).astype(BF)


def prepare(turn, target, patch, weight, atmos, ocean, mask):
    ca, co = atmos.shape[0], ocean.shape[0]
    sm = pl.BlockSpec(memory_space=SMEM)
    whole = lambda shape: pl.BlockSpec(shape, lambda i: (0,) * len(shape))
    shape = jax.ShapeDtypeStruct
    return pl.pallas_call(
        prep_kernel,
        grid=(8,),
        out_shape=(
            shape((S, ca, S), BF),
            shape((S, co, S), BF),
            shape((4, ca, S), BF),
            shape((4, co, S), BF),
            shape((2 * S, CS, S), BF),
            shape((S, 1, S), F32),
            shape((S, CS, S), BF),
            shape((S,), jnp.int32),
        ),
        in_specs=[sm] * 4
        + [
            pl.BlockSpec((ca, 16, S), lambda i: (0, i, 0)),
            whole((CS, S, S)),
            pl.BlockSpec((co, 16, S), lambda i: (0, i, 0)),
            pl.BlockSpec((16, S), lambda i: (i, 0)),
        ],
        out_specs=(
            pl.BlockSpec((16, ca, S), lambda i: (i, 0, 0)),
            pl.BlockSpec((16, co, S), lambda i: (i, 0, 0)),
            whole((4, ca, S)),
            whole((4, co, S)),
            whole((2 * S, CS, S)),
            whole((S, 1, S)),
            whole((S, CS, S)),
            sm,
        ),
        scratch_shapes=[
            VMEM((ca * 16, S), F32),
            VMEM((co * 16, S), F32),
            VMEM((S * CS, S), F32),
            VMEM((2, ca, S), BF),
            VMEM((2, co, S), BF),
            VMEM((4, ca, S), BF),
            VMEM((S, CS, S), BF),
            SMEM((S,), jnp.int32),
            SMEM((2 * S,), jnp.int32),
            SMEM((2 * S,), F32),
        ],
        name="prepare",
    )(turn, target, patch, weight, atmos, atmos, ocean, mask)


def remap_kernel(
    turn_ref, patch_ref, weight_ref, in_ref, common_ref, sea_ref, es_ref, back_ref, total, share, cols
):
    turn = turn_ref[0]
    total[...] = jnp.zeros_like(total)

    def clear(p, _):
        share[p] = 0.0
        return 0

    lax.fori_loop(0, S, clear, 0)

    def gather(i, _):
        for u in range(4):
            n = i * 4 + u
            place, weight = patch_ref[n], weight_ref[n]
            rows = pl.ds(pl.multiple_of(place * CS, CS), CS)
            total[rows, :] = total[rows, :] + weight * in_ref[n].astype(F32)
            share[place] = share[place] + weight
            back_ref[n] = common_ref[place]
        return 0

    lax.fori_loop(0, 2 * S // 4, gather, 0)
    first, last = lanes(CS) == 0, lanes(CS) == S - 1

    def divide(i, _):
        for u in range(4):
            r = i * 4 + u
            rows = pl.ds(pl.multiple_of(r * CS, CS), CS)
            v = (total[rows, :] / jnp.maximum(share[r], 1.0)).astype(BF)
            total[rows, :] = v.astype(F32)
            sea_ref[r] = v
            cols[0] = roll(jnp.where(first, v, cols[0]), -1)
            cols[1] = jnp.where(last, v, roll(cols[1], -1))
        return 0

    lax.fori_loop(0, S // 4, divide, 0)
    es_ref[UP], es_ref[DOWN], es_ref[LEFT], es_ref[RIGHT] = sea_ref[0], sea_ref[S - 1], cols[0], cols[1]
    for quarter in range(1, 4):

        @pl.when(turn == quarter)
        def _():
            for c in range(CS):
                strip = pl.ds(c, S, stride=CS)
                total[strip, :] = turn_matrix(total[strip, :].astype(BF), quarter)
            sea_ref[...] = total[...].reshape(S, CS, S).astype(BF)


def remap(turn, patch, weight, incoming, common):
    sm, vm = pl.BlockSpec(memory_space=SMEM), pl.BlockSpec(memory_space=VMEM)
    shape = jax.ShapeDtypeStruct
    return pl.pallas_call(
        remap_kernel,
        out_shape=(
            shape((S, CS, S), BF),
            shape((4, CS, S), BF),
            shape((2 * S, CS, S), BF),
        ),
        in_specs=[sm] * 3 + [vm] * 2,
        out_specs=(vm,) * 3,
        scratch_shapes=[VMEM((S * CS, S), F32), SMEM((S,), F32), VMEM((2, CS, S), BF)],
        name="remap",
    )(turn, patch, weight, incoming, common)


class Exchange:
    def __init__(self, src, dst, ocean, send, recv, near):
        f, t = lax.axis_index("face"), lax.axis_index("tile")
        n_face, n_tile = lax.axis_size("face"), lax.axis_size("tile")
        fu, fd = (f + n_face - 1) % n_face, (f + 1) % n_face
        tl, tr = (t + n_tile - 1) % n_tile, (t + 1) % n_tile
        copy = lambda n, side, slot, device: pltpu.make_async_remote_copy(
            src_ref=src.at[side],
            dst_ref=dst.at[slot],
            send_sem=send.at[n],
            recv_sem=recv.at[slot],
            device_id=device,
            device_id_type=MESH,
        )
        always, top, bottom = None, f > 0, f < n_face - 1
        if not ocean:
            top = bottom = None
        self.copies = [
            (always, copy(0, LEFT, RIGHT, (f, tl))),
            (always, copy(1, RIGHT, LEFT, (f, tr))),
            (top, copy(2, UP, DOWN, (fu, t))),
            (top, copy(3, UP, DR, (fu, tl))),
            (top, copy(4, UP, DL, (fu, tr))),
            (bottom, copy(5, DOWN, UP, (fd, t))),
            (bottom, copy(6, DOWN, UR, (fd, tl))),
            (bottom, copy(7, DOWN, UL, (fd, tr))),
        ]
        self.local = []
        self.arrivals = [(None, LEFT), (None, RIGHT)]
        if ocean:
            fold = f == n_face - 1
            inner = fold & (lax.rem(t, n_tile // 2) != 0)
            outer = fold & (lax.rem(t, n_tile // 2) != n_tile // 2 - 1)
            left_to, right_to = (2 * n_tile - t) % n_tile, (2 * n_tile - 2 - t) % n_tile
            self.copies += [
                (fold, copy(5, DOWN, DOWN, (f, n_tile - 1 - t))),
                (inner, copy(6, DOWN, DL, (f, left_to))),
                (outer, copy(7, DOWN, DR, (f, right_to))),
            ]
            own_left = fold & (lax.rem(t, n_tile // 2) == 0)
            own_right = fold & (lax.rem(t, n_tile // 2) == n_tile // 2 - 1)
            self.local = [
                (own_left, pltpu.make_async_copy(src.at[DOWN], dst.at[DL], near)),
                (own_right, pltpu.make_async_copy(src.at[DOWN], dst.at[DR], near)),
            ]
            self.arrivals += [(top, UP), (top, UL), (top, UR), (None, DOWN)]
            self.arrivals += [(bottom | inner, DL), (bottom | outer, DR)]
        else:
            self.arrivals += [(None, n) for n in (UP, DOWN, UL, UR, DL, DR)]
        self.arrived = lambda slot: copy(0, LEFT, slot, (f, tl)).wait_recv()

    @staticmethod
    def given(condition, act):
        if condition is None:
            act()
        else:
            pl.when(condition)(act)

    def start(self):
        for condition, each in self.copies + self.local:
            self.given(condition, each.start)

    def wait(self):
        for condition, slot in self.arrivals:
            self.given(condition, partial(self.arrived, slot))
        for condition, each in self.local:
            self.given(condition, each.wait)
        for condition, each in self.copies:
            self.given(condition, each.wait_send)


def place():
    f, t = lax.axis_index("face"), lax.axis_index("tile")
    n_tile = lax.axis_size("tile")
    return f * n_tile + t, lax.axis_size("face") * n_tile, n_tile


def meet_all():
    me, count, n_tile = place()
    barrier = pltpu.get_barrier_semaphore()

    def greet(i, _):
        peer = (me + i) % count
        pl.semaphore_signal(barrier, inc=1, device_id=(peer // n_tile, peer % n_tile), device_id_type=MESH)
        return 0

    lax.fori_loop(1, count, greet, 0)
    pl.semaphore_wait(barrier, count - 1)


def meet_around():
    f, t = lax.axis_index("face"), lax.axis_index("tile")
    n_face, n_tile = lax.axis_size("face"), lax.axis_size("tile")
    barrier = pltpu.get_barrier_semaphore()

    def greet(face, tile):
        pl.semaphore_signal(barrier, inc=1, device_id=(face, tile), device_id_type=MESH)

    for df in (n_face - 1, 0, 1):
        for dt in (n_tile - 1, 0, 1):
            if df or dt:
                greet((f + df) % n_face, (t + dt) % n_tile)
    fold = f == n_face - 1
    half = n_tile // 2
    inner = fold & (lax.rem(t, half) != 0)
    outer = fold & (lax.rem(t, half) != half - 1)
    pl.when(fold)(lambda: greet(f, n_tile - 1 - t))
    pl.when(inner)(lambda: greet(f, (2 * n_tile - t) % n_tile))
    pl.when(outer)(lambda: greet(f, (2 * n_tile - 2 - t) % n_tile))
    more = [jnp.where(condition, 1, 0) for condition in (fold, inner, outer)]
    pl.semaphore_wait(barrier, 8 + more[0] + more[1] + more[2])


def everyone(src, dst, rows, send, recv, near):
    me, count, n_tile = place()

    def copy(peer):
        return pltpu.make_async_remote_copy(
            src_ref=src.at[pl.ds(peer * rows, rows)],
            dst_ref=dst.at[pl.ds(me * rows, rows)],
            send_sem=send,
            recv_sem=recv,
            device_id=(peer // n_tile, peer % n_tile),
            device_id_type=MESH,
        )

    own = pltpu.make_async_copy(src.at[pl.ds(me * rows, rows)], dst.at[pl.ds(me * rows, rows)], near)
    other = (lax.axis_index("face"), (lax.axis_index("tile") + 1) % n_tile)
    rest = pltpu.make_async_remote_copy(
        src_ref=src.at[pl.ds(0, (count - 1) * rows)],
        dst_ref=dst.at[pl.ds(0, (count - 1) * rows)],
        send_sem=send,
        recv_sem=recv,
        device_id=other,
        device_id_type=MESH,
    )

    def start():
        def one(i, _):
            copy((me + i) % count).start()
            return 0

        lax.fori_loop(1, count, one, 0)
        own.start()

    def wait():
        own.wait()
        rest.wait_recv()
        rest.wait_send()

    return start, wait


def first_kernel(pay, meta, ea, eo, pay_in, meta_in, ha, ho, wide, flat, sa, ra, so, ro, near):
    meet_all()
    start_meta, wait_meta = everyone(meta, meta_in, 1, wide.at[0], wide.at[1], near.at[0])
    start_pay, wait_pay = everyone(pay, pay_in, 2, flat.at[0], flat.at[1], near.at[1])
    atmos = Exchange(ea, ha, False, sa, ra, near.at[2])
    ocean = Exchange(eo, ho, True, so, ro, near.at[2])
    start_meta()
    start_pay()
    atmos.start()
    ocean.start()
    wait_meta()
    wait_pay()
    atmos.wait()
    ocean.wait()


DMA = pltpu.SemaphoreType.DMA
EIGHT = [DMA((8,))] * 4


def first_exchange(pay, meta, ea, eo):
    hbm = pl.BlockSpec(memory_space=pl.ANY)
    shape = jax.ShapeDtypeStruct
    return pl.pallas_call(
        first_kernel,
        out_shape=(
            shape(pay.shape, BF),
            shape(meta.shape, F32),
            shape((8, *ea.shape[1:]), BF),
            shape((8, *eo.shape[1:]), BF),
        ),
        in_specs=[hbm] * 4,
        out_specs=(hbm,) * 4,
        scratch_shapes=[DMA((2,)), DMA((2,))] + EIGHT + [DMA((3,))],
        compiler_params=pltpu.CompilerParams(collective_id=0, has_side_effects=True),
        name="first_exchange",
    )(pay, meta, ea, eo)


def second_kernel(slot_ref, back, es, hs, force_ref, hf, got, own, cols, flat, sa, ra, so, ro, near):
    meet_all()
    start_back, wait_back = everyone(back, got, 2, flat.at[0], flat.at[1], near.at[0])
    sea = Exchange(es, hs, False, sa, ra, near.at[1])
    sea.start()
    start_back()
    wait_back()
    first, last = lanes(CS) == 0, lanes(CS) == S - 1

    def put(i, _):
        for u in range(4):
            b = i * 4 + u
            v = got[slot_ref[b]]
            force_ref[b] = v
            cols[0] = roll(jnp.where(first, v, cols[0]), -1)
            cols[1] = jnp.where(last, v, roll(cols[1], -1))
        return 0

    lax.fori_loop(0, S // 4, put, 0)
    own[UP], own[DOWN], own[LEFT], own[RIGHT] = force_ref[0], force_ref[S - 1], cols[0], cols[1]
    sea.wait()
    force = Exchange(own, hf, True, so, ro, near.at[1])
    force.start()
    force.wait()


def second_exchange(slots, back, es):
    hbm, vm, sm = (pl.BlockSpec(memory_space=m) for m in (pl.ANY, VMEM, SMEM))
    shape = jax.ShapeDtypeStruct
    return pl.pallas_call(
        second_kernel,
        out_shape=(
            shape((8, CS, S), BF),
            shape((S, CS, S), BF),
            shape((8, CS, S), BF),
        ),
        in_specs=[sm, hbm, hbm],
        out_specs=(hbm, vm, hbm),
        scratch_shapes=[VMEM((2 * S, CS, S), BF), VMEM((4, CS, S), BF), VMEM((2, CS, S), BF), DMA((2,))]
        + EIGHT
        + [DMA((2,))],
        compiler_params=pltpu.CompilerParams(collective_id=1, has_side_effects=True),
        name="second_exchange",
    )(slots, back, es)


def third_kernel(ea, eo, ha, ho, sa, ra, so, ro, near):
    meet_around()
    atmos = Exchange(ea, ha, False, sa, ra, near)
    ocean = Exchange(eo, ho, True, so, ro, near)
    atmos.start()
    ocean.start()
    atmos.wait()
    ocean.wait()


def third_exchange(ea, eo):
    hbm = pl.BlockSpec(memory_space=pl.ANY)
    shape = jax.ShapeDtypeStruct
    return pl.pallas_call(
        third_kernel,
        out_shape=(
            shape((8, *ea.shape[1:]), BF),
            shape((8, *eo.shape[1:]), BF),
        ),
        in_specs=[hbm] * 2,
        out_specs=(hbm,) * 2,
        scratch_shapes=EIGHT + [DMA],
        compiler_params=pltpu.CompilerParams(collective_id=2, has_side_effects=True),
        name="third_exchange",
    )(ea, eo)


def taps(weight):
    _, outs, channels = weight.shape
    return weight.reshape(3, 3, outs, channels).transpose(0, 2, 1, 3).reshape(3 * outs, 3 * channels)


TURNED_TAPS = (
    (0, 1, 2, 3, 4, 5, 6, 7, 8),
    (2, 5, 8, 1, 4, 7, 0, 3, 6),
    (8, 7, 6, 5, 4, 3, 2, 1, 0),
    (6, 3, 0, 7, 4, 1, 8, 5, 2),
)


def on_device(
    atmos_state, ocean_state, land_mask, face_turns, block_target, block_patch, block_weight,
    atmos_w1, atmos_w2, ocean_w1, ocean_w2,
):
    turn = face_turns.reshape(1)
    face = lax.axis_index("face")
    edge = jnp.where(face == 0, 1, jnp.where(face == lax.axis_size("face") - 1, 2, 0))
    edge = edge.astype(jnp.int32).reshape(1)
    mask = jnp.repeat(land_mask, 32, axis=1).astype(BF)
    order = jnp.array(TURNED_TAPS, jnp.int32)[turn[0]]
    wa1 = taps(jnp.take(atmos_w1, order, axis=0))
    wa2 = taps(jnp.take(atmos_w2, order, axis=0))
    wo1, wo2 = taps(ocean_w1), taps(ocean_w2)
    weight = lax.reduce_precision(block_weight[:, 0], 8, 7)
    xa, xo, ea, eo, pay, meta, common, slots = prepare(
        turn, block_target[:, 0], block_patch[:, 0], weight, atmos_state, ocean_state, mask
    )
    pay_in, meta_in, ha, ho = first_exchange(pay, meta, ea, eo)
    patch_in = meta_in[:, 0, :2].reshape(2 * S).astype(jnp.int32)
    weight_in = meta_in[:, 0, 2:4].reshape(2 * S)
    sea, es, back = remap(turn, patch_in, weight_in, pay_in, common)
    hs, force, hf = second_exchange(slots, back, es)
    hid_a, ea2 = hidden_conv(False, turn, [xa, sea], [ha, hs], wa1, 16)
    hid_o, eo2 = hidden_conv(True, edge, [xo, force], [ho, hf], wo1, 16)
    ha2, ho2 = third_exchange(ea2, eo2)
    atmos_out = out_conv(False, turn, hid_a, ha2, wa2, atmos_state, mask, 8)
    ocean_out = out_conv(True, edge, hid_o, ho2, wo2, ocean_state, mask, 8)
    return atmos_out, ocean_out


def solution(mesh):
    placed = (
        P(None, "face", "tile"),
        P(None, "face", "tile"),
        P("face", "tile"),
        P("face", "tile"),
        P(("face", "tile"), None),
        P(("face", "tile"), None),
        P(("face", "tile"), None),
        P(),
        P(),
        P(),
        P(),
    )
    return jax.shard_map(
        on_device,
        mesh=mesh,
        in_specs=placed,
        out_specs=(P(None, "face", "tile"), P(None, "face", "tile")),
        check_vma=False,
    )
```

```python
from functools import partial

import jax
import jax.numpy as jnp
from jax import lax
from jax.experimental import pallas as pl
from jax.experimental.pallas import tpu as pltpu
from jax.sharding import PartitionSpec as P

BF = jnp.bfloat16
F32 = jnp.float32
S = 128
CS = 16
MESH = pl.DeviceIdType.MESH
VMEM = pltpu.VMEM
SMEM = pltpu.SMEM

UP, DOWN, LEFT, RIGHT, UL, UR, DL, DR = range(8)
TO_STORED = (
    ((UP, 0), (RIGHT, 0), (DOWN, 1), (LEFT, 1)),
    ((DOWN, 0), (LEFT, 0), (UP, 1), (RIGHT, 1)),
    ((LEFT, 0), (UP, 1), (RIGHT, 1), (DOWN, 0)),
    ((RIGHT, 0), (DOWN, 1), (LEFT, 1), (UP, 0)),
    ((UL, 0), (UR, 1), (DR, 1), (DL, 0)),
    ((UR, 0), (DR, 0), (DL, 1), (UL, 1)),
    ((DL, 0), (UL, 0), (UR, 1), (DR, 1)),
    ((DR, 0), (DL, 1), (UL, 1), (UR, 0)),
)
TO_COMMON = (
    ((UP, 0), (LEFT, 1), (DOWN, 1), (RIGHT, 0)),
    ((DOWN, 0), (RIGHT, 1), (UP, 1), (LEFT, 0)),
    ((LEFT, 0), (DOWN, 0), (RIGHT, 1), (UP, 1)),
    ((RIGHT, 0), (UP, 0), (LEFT, 1), (DOWN, 1)),
)


def anti():
    rows = lax.broadcasted_iota(jnp.int32, (S, S), 0)
    cols = lax.broadcasted_iota(jnp.int32, (S, S), 1)
    return jnp.where(rows + cols == S - 1, 1.0, 0.0).astype(BF)


def eye():
    rows = lax.broadcasted_iota(jnp.int32, (S, S), 0)
    cols = lax.broadcasted_iota(jnp.int32, (S, S), 1)
    return jnp.where(rows == cols, 1.0, 0.0).astype(BF)


def dot(a, b):
    return jnp.dot(a, b, preferred_element_type=F32)


def dot_nt(a, b):
    return lax.dot_general(a, b, (((1,), (1,)), ((), ())), preferred_element_type=F32)


def roll(v, shift):
    return pltpu.roll(v, shift % S, 1)


def lanes(channels):
    return lax.broadcasted_iota(jnp.int32, (channels, S), 1)


def reversed_lanes(v):
    return dot(v, anti()).astype(BF)


def select_sides(table, mode, source, target):
    for turn in range(4):

        @pl.when(mode == turn)
        def _():
            for i, row in enumerate(table):
                side, flip = row[turn]
                v = source[side]
                target[i] = reversed_lanes(v) if flip else v


def ocean_sides(mode, source, target):
    for i in range(8):
        target[i] = source[i]

    @pl.when(mode == 1)
    def _():
        for i in (UP, UL, UR):
            target[i] = jnp.zeros_like(target[i])

    @pl.when(mode == 2)
    def _():
        for i in (DOWN, DL, DR):
            target[i] = reversed_lanes(source[i])


def blended_sides(table, mode, source, flipped, target):
    count, channels = source.shape[0], source.shape[1]
    flat = source[...].reshape(count * channels, S)
    flipped[:count] = reversed_lanes(flat).reshape(count, channels, S)
    for i, row in enumerate(table):
        v = None
        for turn, (side, flip) in enumerate(row):
            each = flipped[side] if flip else source[side]
            v = each if v is None else jnp.where(mode == turn, each, v)
        target[i] = v


def folded_sides(source, target):
    f, n_face = lax.axis_index("face"), lax.axis_size("face")
    target[LEFT], target[RIGHT] = source[LEFT], source[RIGHT]
    for i in (UP, UL, UR):

        @pl.when(f == 0)
        def _():
            target[i] = jnp.zeros(target.shape[1:], BF)

        @pl.when(f > 0)
        def _():
            target[i] = source[i]

    for i in (DOWN, DL, DR):

        @pl.when(f == n_face - 1)
        def _():
            target[i] = reversed_lanes(source[i])

        @pl.when(f < n_face - 1)
        def _():
            target[i] = source[i]


def turn_matrix(v, turns):
    if turns == 1:
        return dot_nt(anti(), v)
    if turns == 2:
        return dot(dot(anti(), v).astype(BF), anti())
    if turns == 3:
        return dot_nt(eye(), dot(anti(), v).astype(BF))
    return v.astype(F32)


def conv_rows(parts, sides, runs, w_ref, outs, carry, finish, flush, unroll):
    first = [lanes(p.shape[1]) == 0 for p in parts]
    last = [lanes(p.shape[1]) == S - 1 for p in parts]
    for side, run in zip(sides, runs):
        run[0] = side[LEFT]
        run[1] = roll(side[LEFT], 64)
        run[2] = roll(side[RIGHT], 1)
        run[3] = roll(side[RIGHT], 65)

    def products(r, first_row, end):
        left, centre, right = [], [], []
        for n, (p, side, run) in enumerate(zip(parts, sides, runs)):
            la, lb, ra, rb = run[0], run[1], run[2], run[3]
            run[0], run[1], run[2], run[3] = roll(la, -1), roll(lb, -1), roll(ra, -1), roll(rb, -1)
            if first_row:
                xa, la, ra = side[UP], side[UL], side[UR]
            else:
                xa = p[r - 1]
            if end is None:
                xb = p[r + 63]
            else:
                xb = jnp.where(end, side[DOWN], p[jnp.minimum(r + 63, S - 1)])
                lb, rb = jnp.where(end, side[DL], lb), jnp.where(end, side[DR], rb)
            both = lambda a, b: jnp.concatenate([a, b], axis=1)
            left.append(both(roll(jnp.where(last[n], la, xa), 1), roll(jnp.where(last[n], lb, xb), 1)))
            centre.append(both(xa, xb))
            right.append(both(roll(jnp.where(first[n], ra, xa), -1), roll(jnp.where(first[n], rb, xb), -1)))
        return dot(w_ref[...], jnp.concatenate(left + centre + right, axis=0))

    o = outs
    p0 = products(0, True, None)
    p1 = products(1, False, None)
    carry[0] = p0[:o] + p1[o : 2 * o]
    carry[1] = p1[:o]

    def sixteen(g, _):
        def body(i, _):
            done, near = carry[0], carry[1]
            for u in range(unroll):
                y = g * 16 + i * unroll + u
                p = products(y + 2, False, y == 63 if u == unroll - 1 else None)
                finish(y, done + p[2 * o :])
                done, near = near + p[o : 2 * o], p[:o]
            carry[0], carry[1] = done, near
            return 0

        lax.fori_loop(0, 16 // unroll, body, 0)
        if flush is not None:
            flush(g)
        return 0

    lax.fori_loop(0, 4, sixteen, 0)


def hidden_rows(parts, sides, runs, w_ref, hid_ref, carry, cols, own, unroll):
    outs = hid_ref.shape[1]
    first, last = lanes(outs) == 0, lanes(outs) == S - 1

    def finish(y, both):
        for half in range(2):
            v = jax.nn.gelu(both[:, half * S : (half + 1) * S], approximate=True).astype(BF)
            hid_ref[y + 64 * half] = v
            cols[half] = roll(jnp.where(first, v, cols[half]), -1)
            cols[2 + half] = jnp.where(last, v, roll(cols[2 + half], -1))

    conv_rows(parts, sides, runs, w_ref, outs, carry, finish, None, unroll)
    upper = lanes(outs) >= 64
    own[UP], own[DOWN] = hid_ref[0], hid_ref[S - 1]
    own[LEFT] = jnp.where(upper, cols[1], roll(cols[0], 64))
    own[RIGHT] = jnp.where(upper, cols[3], roll(cols[2], 64))


def out_kernel(ocean, unroll, mode_ref, hid_ref, halo_ref, w_ref, base_ref, mask_ref, out_ref, side, run, carry, stage):
    mode = mode_ref[0]
    if ocean:
        ocean_sides(mode, halo_ref, side)
    else:
        select_sides(TO_STORED, mode, halo_ref, side)
    outs = hid_ref.shape[1]

    def finish(y, both):
        place = lax.rem(y, 16)
        for half in range(2):
            stage[half, pl.ds(place, outs, stride=16), :] = both[:, half * S : (half + 1) * S]

    def flush(g):
        for half in range(2):
            rows = pl.ds(pl.multiple_of(g * 16 + 64 * half, 16), 16)
            base = base_ref[:, rows, :].astype(F32)
            summed = stage[half].reshape(outs, 16, S)
            if ocean:
                gate = mask_ref[rows, :].astype(F32)[None]
                out_ref[:, rows, :] = (gate * (gate * base + summed)).astype(BF)
            else:
                out_ref[:, rows, :] = (base + summed).astype(BF)

    conv_rows([hid_ref], [side], [run], w_ref, outs, carry, finish, flush, unroll)


def out_conv(ocean, mode, hidden, halo, weight, base, mask, unroll):
    outs = hidden.shape[1]
    vm = pl.BlockSpec(memory_space=VMEM)
    return pl.pallas_call(
        partial(out_kernel, ocean, unroll),
        out_shape=jax.ShapeDtypeStruct((outs, S, S), BF),
        in_specs=[pl.BlockSpec(memory_space=SMEM)] + [vm] * 5,
        out_specs=vm,
        scratch_shapes=[
            VMEM((8, outs, S), BF),
            VMEM((4, outs, S), BF),
            VMEM((2, outs, 2 * S), F32),
            VMEM((2, outs * 16, S), F32),
        ],
        name="out_ocean" if ocean else "out_atmos",
    )(mode, hidden, halo, weight, base, mask)


def prep_kernel(
    turn_ref, target_ref, patch_ref, weight_ref, atmos_ref, ocean_ref, mask_ref,
    pay_ref, meta_ref, common_ref, slot_ref, surf, tally,
):
    turn = turn_ref[0]
    gate = mask_ref[...].astype(F32)[None]
    surf[...] = jnp.swapaxes((ocean_ref[...].astype(F32) * gate).astype(BF), 0, 1)
    pay_ref[...] = jnp.zeros_like(pay_ref)
    meta_ref[...] = jnp.zeros_like(meta_ref)

    def clear(i, _):
        for u in range(8):
            tally[i * 8 + u] = 0
        return 0

    lax.fori_loop(0, S // 8, clear, 0)
    lane = lanes(1)

    def place(i, _):
        for u in range(4):
            b = i * 4 + u
            goal = target_ref[b]
            seen = tally[goal]
            slot = 2 * goal + seen
            tally[goal] = seen + 1
            slot_ref[b] = slot
            pay_ref[slot] = surf[b]
            spot = jnp.full((1, S), patch_ref[b], jnp.int32).astype(F32)
            meta_ref[slot] = jnp.where(lane == 0, spot, weight_ref[b])
        return 0

    lax.fori_loop(0, S // 4, place, 0)
    for quarter in range(4):

        @pl.when(turn == quarter)
        def _():
            for c in range(CS):
                common_ref[c] = turn_matrix(atmos_ref[c], (4 - quarter) % 4).astype(BF)


def prepare(turn, target, patch, weight, atmos, ocean, mask):
    sm = pl.BlockSpec(memory_space=SMEM)
    head = pl.BlockSpec((CS, S, S), lambda i: (0, 0, 0))
    whole = lambda shape: pl.BlockSpec(shape, lambda i: (0,) * len(shape))
    shape = jax.ShapeDtypeStruct
    return pl.pallas_call(
        prep_kernel,
        grid=(1,),
        out_shape=(
            shape((2 * S, CS, S), BF),
            shape((2 * S, 1, S), F32),
            shape((CS, S, S), BF),
            shape((S,), jnp.int32),
        ),
        in_specs=[sm] * 4 + [head, head, whole((S, S))],
        out_specs=(whole((2 * S, CS, S)), whole((2 * S, 1, S)), whole((CS, S, S)), sm),
        scratch_shapes=[VMEM((S, CS, S), BF), SMEM((S,), jnp.int32)],
        name="prepare",
    )(turn, target, patch, weight, atmos, ocean, mask)


def remap_kernel(
    turn_ref, meta_ref, in_ref, common_ref, sea_ref, es_ref, back_ref, wide, total, spread
):
    turn = turn_ref[0]
    meta = meta_ref[...].reshape(2 * S, S)
    spot = jnp.broadcast_to(meta[:, 0:1], (2 * S, S))
    share = jnp.broadcast_to(meta[:, 1:2], (2 * S, S))
    faces = spot == lax.broadcasted_iota(jnp.int32, (2 * S, S), 1).astype(F32)
    pick = jnp.where(faces, 1.0, 0.0).astype(BF)
    spread[...] = dot_nt(eye(), jnp.where(faces, share, 0.0).astype(BF)).astype(BF)
    amount = jnp.maximum(dot(spread[...], jnp.ones((2 * S, S), BF)), 1.0)
    wide[...] = in_ref[...].astype(F32).reshape(wide.shape)
    sides = lax.broadcasted_iota(jnp.int32, (16, S), 0)
    along = lax.broadcasted_iota(jnp.int32, (16, S), 1)
    ends = jnp.where(along == jnp.where(sides < 2, sides * (S - 1), -1), 1.0, 0.0).astype(BF)
    for c in range(CS):
        strip = pl.ds(c, 2 * S, stride=CS)
        blocks = wide[strip, :].astype(BF)
        v = (dot(spread[...], blocks) / amount).astype(BF)
        wide[strip, :] = dot(pick, common_ref[c])
        total[pl.ds(c, S, stride=CS), :] = v.astype(F32)
        edge = dot_nt(ends, v)
        es_ref[LEFT, pl.ds(c, 1), :] = edge[0:1]
        es_ref[RIGHT, pl.ds(c, 1), :] = edge[1:2]
    back_ref[...] = wide[...].reshape(2 * S, CS, S).astype(BF)
    es_ref[UP] = total[pl.ds(0, CS), :]
    es_ref[DOWN] = total[pl.ds((S - 1) * CS, CS), :]
    for quarter in range(1, 4):

        @pl.when(turn == quarter)
        def _():
            for c in range(CS):
                strip = pl.ds(c, S, stride=CS)
                total[strip, :] = turn_matrix(total[strip, :].astype(BF), quarter)

    sea_ref[...] = total[...].reshape(S, CS, S).astype(BF)


def remap(turn, meta, incoming, common):
    sm, vm = pl.BlockSpec(memory_space=SMEM), pl.BlockSpec(memory_space=VMEM)
    shape = jax.ShapeDtypeStruct
    return pl.pallas_call(
        remap_kernel,
        out_shape=(
            shape((S, CS, S), BF),
            shape((4, CS, S), F32),
            shape((2 * S, CS, S), BF),
        ),
        in_specs=[sm] + [vm] * 3,
        out_specs=(vm,) * 3,
        scratch_shapes=[VMEM((2 * S * CS, S), F32), VMEM((S * CS, S), F32), VMEM((S, 2 * S), BF)],
        name="remap",
    )(turn, meta, incoming, common)


class Exchange:
    def __init__(self, src, dst, ocean, send, recv, near):
        f, t = lax.axis_index("face"), lax.axis_index("tile")
        n_face, n_tile = lax.axis_size("face"), lax.axis_size("tile")
        fu, fd = (f + n_face - 1) % n_face, (f + 1) % n_face
        tl, tr = (t + n_tile - 1) % n_tile, (t + 1) % n_tile
        copy = lambda n, side, slot, device: pltpu.make_async_remote_copy(
            src_ref=src.at[side],
            dst_ref=dst.at[slot],
            send_sem=send.at[n],
            recv_sem=recv.at[slot],
            device_id=device,
            device_id_type=MESH,
        )
        always, top, bottom = None, f > 0, f < n_face - 1
        if not ocean:
            top = bottom = None
        self.copies = [
            (always, copy(0, LEFT, RIGHT, (f, tl))),
            (always, copy(1, RIGHT, LEFT, (f, tr))),
            (top, copy(2, UP, DOWN, (fu, t))),
            (top, copy(3, UP, DR, (fu, tl))),
            (top, copy(4, UP, DL, (fu, tr))),
            (bottom, copy(5, DOWN, UP, (fd, t))),
            (bottom, copy(6, DOWN, UR, (fd, tl))),
            (bottom, copy(7, DOWN, UL, (fd, tr))),
        ]
        self.local = []
        self.arrivals = [(None, LEFT), (None, RIGHT)]
        if ocean:
            fold = f == n_face - 1
            inner = fold & (lax.rem(t, n_tile // 2) != 0)
            outer = fold & (lax.rem(t, n_tile // 2) != n_tile // 2 - 1)
            left_to, right_to = (2 * n_tile - t) % n_tile, (2 * n_tile - 2 - t) % n_tile
            self.copies += [
                (fold, copy(5, DOWN, DOWN, (f, n_tile - 1 - t))),
                (inner, copy(6, DOWN, DL, (f, left_to))),
                (outer, copy(7, DOWN, DR, (f, right_to))),
            ]
            own_left = fold & (lax.rem(t, n_tile // 2) == 0)
            own_right = fold & (lax.rem(t, n_tile // 2) == n_tile // 2 - 1)
            self.local = [
                (own_left, pltpu.make_async_copy(src.at[DOWN], dst.at[DL], near)),
                (own_right, pltpu.make_async_copy(src.at[DOWN], dst.at[DR], near)),
            ]
            self.arrivals += [(top, UP), (top, UL), (top, UR), (None, DOWN)]
            self.arrivals += [(bottom | inner, DL), (bottom | outer, DR)]
        else:
            self.arrivals += [(None, n) for n in (UP, DOWN, UL, UR, DL, DR)]
        self.arrived = lambda slot: copy(0, LEFT, slot, (f, tl)).wait_recv()

    @staticmethod
    def given(condition, act):
        if condition is None:
            act()
        else:
            pl.when(condition)(act)

    def start(self):
        for condition, each in self.copies + self.local:
            self.given(condition, each.start)

    def wait(self):
        for condition, slot in self.arrivals:
            self.given(condition, partial(self.arrived, slot))
        for condition, each in self.local:
            self.given(condition, each.wait)
        for condition, each in self.copies:
            self.given(condition, each.wait_send)


def place():
    f, t = lax.axis_index("face"), lax.axis_index("tile")
    n_tile = lax.axis_size("tile")
    return f * n_tile + t, lax.axis_size("face") * n_tile, n_tile


def meet_all():
    me, count, n_tile = place()
    barrier = pltpu.get_barrier_semaphore()

    def greet(i, _):
        peer = (me + i) % count
        pl.semaphore_signal(barrier, inc=1, device_id=(peer // n_tile, peer % n_tile), device_id_type=MESH)
        return 0

    lax.fori_loop(1, count, greet, 0)
    pl.semaphore_wait(barrier, count - 1)


def everyone(src, dst, rows, send, recv, near):
    me, count, n_tile = place()

    def copy(peer):
        return pltpu.make_async_remote_copy(
            src_ref=src.at[pl.ds(peer * rows, rows)],
            dst_ref=dst.at[pl.ds(me * rows, rows)],
            send_sem=send,
            recv_sem=recv,
            device_id=(peer // n_tile, peer % n_tile),
            device_id_type=MESH,
        )

    own = pltpu.make_async_copy(src.at[pl.ds(me * rows, rows)], dst.at[pl.ds(me * rows, rows)], near)
    other = (lax.axis_index("face"), (lax.axis_index("tile") + 1) % n_tile)
    rest = pltpu.make_async_remote_copy(
        src_ref=src.at[pl.ds(0, (count - 1) * rows)],
        dst_ref=dst.at[pl.ds(0, (count - 1) * rows)],
        send_sem=send,
        recv_sem=recv,
        device_id=other,
        device_id_type=MESH,
    )

    def start():
        def one(i, _):
            copy((me + i) % count).start()
            return 0

        lax.fori_loop(1, count, one, 0)
        own.start()

    def wait():
        own.wait()
        rest.wait_recv()
        rest.wait_send()

    return start, wait


DMA = pltpu.SemaphoreType.DMA
EIGHT = [DMA((8,))] * 4


def first_kernel(
    turn_ref, mask_ref, pay, meta, atmos, ocean, pay_in, meta_in, xa_ref, xo_ref, ha, ho,
    held_a, held_o, wide_a, wide_o, cols_a, cols_o, own_a, flip_a, side_a, own_o,
    loads, wide, flat, sa, ra, so, ro, near,
):
    def load(g, n):
        source, held = ((atmos, held_a), (ocean, held_o))[n]
        rows = pl.ds(pl.multiple_of(g * 16, 16), 16)
        return pltpu.make_async_copy(source.at[:, rows, :], held.at[g], loads.at[n, g])

    for n in range(2):
        for g in range(8):
            load(g, n).start()
    meet_all()
    start_meta, wait_meta = everyone(meta, meta_in, 2, wide.at[0], wide.at[1], near.at[0])
    start_pay, wait_pay = everyone(pay, pay_in, 2, flat.at[0], flat.at[1], near.at[1])
    start_meta()
    start_pay()

    def columns(cols, v):
        first, last = lanes(v.shape[0]) == 0, lanes(v.shape[0]) == S - 1
        cols[0] = roll(jnp.where(first, v, cols[0]), -1)
        cols[1] = jnp.where(last, v, roll(cols[1], -1))

    def sixteen(g, _):
        for n in range(2):
            load(g, n).wait()
        rows = pl.ds(pl.multiple_of(g * 16, 16), 16)
        wide_a[...] = held_a[g].astype(F32).reshape(wide_a.shape)
        gate = mask_ref[rows, :].astype(F32)[None]
        wide_o[...] = (held_o[g].astype(F32) * gate).reshape(wide_o.shape)
        for y in range(16):
            v = wide_a[pl.ds(y, wide_a.shape[0] // 16, stride=16), :].astype(BF)
            xa_ref[g * 16 + y] = v
            columns(cols_a, v)
            v = wide_o[pl.ds(y, wide_o.shape[0] // 16, stride=16), :].astype(BF)
            xo_ref[g * 16 + y] = v
            columns(cols_o, v)
        return 0

    cols_a[...] = jnp.zeros_like(cols_a)
    cols_o[...] = jnp.zeros_like(cols_o)
    lax.fori_loop(0, 8, sixteen, 0)
    own_a[UP], own_a[DOWN], own_a[LEFT], own_a[RIGHT] = xa_ref[0], xa_ref[S - 1], cols_a[0], cols_a[1]
    own_o[UP], own_o[DOWN], own_o[LEFT], own_o[RIGHT] = xo_ref[0], xo_ref[S - 1], cols_o[0], cols_o[1]
    blended_sides(TO_COMMON, turn_ref[0], own_a, flip_a, side_a)
    at = Exchange(side_a, ha, False, sa, ra, near.at[2])
    oc = Exchange(own_o, ho, True, so, ro, near.at[2])
    at.start()
    oc.start()
    wait_meta()
    wait_pay()
    at.wait()
    oc.wait()


def first_exchange(turn, mask, pay, meta, atmos, ocean):
    hbm, vm, sm = (pl.BlockSpec(memory_space=m) for m in (pl.ANY, VMEM, SMEM))
    shape = jax.ShapeDtypeStruct
    ca, co = atmos.shape[0], ocean.shape[0]
    return pl.pallas_call(
        first_kernel,
        out_shape=(
            shape(pay.shape, BF),
            shape(meta.shape, F32),
            shape((S, ca, S), BF),
            shape((S, co, S), BF),
            shape((8, ca, S), BF),
            shape((8, co, S), BF),
        ),
        in_specs=[sm, vm] + [hbm] * 4,
        out_specs=(hbm, hbm, vm, vm, hbm, hbm),
        scratch_shapes=[
            VMEM((8, ca, 16, S), BF),
            VMEM((8, co, 16, S), BF),
            VMEM((ca * 16, S), F32),
            VMEM((co * 16, S), F32),
            VMEM((2, ca, S), BF),
            VMEM((2, co, S), BF),
            VMEM((4, ca, S), BF),
            VMEM((4, ca, S), BF),
            VMEM((4, ca, S), BF),
            VMEM((4, co, S), BF),
            DMA((2, 8)),
            DMA((2,)),
            DMA((2,)),
        ]
        + EIGHT
        + [DMA((3,))],
        compiler_params=pltpu.CompilerParams(collective_id=0, has_side_effects=True),
        name="first_exchange",
    )(turn, mask, pay, meta, atmos, ocean)


def second_kernel(
    unroll, slot_ref, turn_ref, back, es, xa, xo, sea_ref, ha_ref, ho_ref, wa_ref, wo_ref,
    hid_a, hid_o, ha2, ho2,
    x_a, x_o, hs, hf, got, force, flip, flip_s, sides_a, sides_s, sides_o, sides_f,
    run_a, run_s, run_o, run_f, carry_a, carry_o, cols_a, cols_o, cols_f, own_a, out_a, own_o, own_f,
    loads, flat, sem_s, sem_f, sem_a, sem_o, near,
):
    turn = turn_ref[0]
    load_a = pltpu.make_async_copy(xa, x_a, loads.at[0])
    load_o = pltpu.make_async_copy(xo, x_o, loads.at[1])
    load_a.start()
    load_o.start()
    meet_all()
    start_back, wait_back = everyone(back, got, 2, flat.at[0], flat.at[1], near.at[0])
    sea = Exchange(es, hs, False, sem_s.at[0], sem_s.at[1], near.at[1])
    sea.start()
    start_back()
    blended_sides(TO_STORED, turn, ha_ref, flip, sides_a)
    folded_sides(ho_ref, sides_o)
    load_a.wait()
    sea.wait()
    blended_sides(TO_STORED, turn, hs, flip_s, sides_s)
    cols_a[...] = jnp.zeros_like(cols_a)
    cols_o[...] = jnp.zeros_like(cols_o)
    cols_f[...] = jnp.zeros_like(cols_f)
    hidden_rows([x_a, sea_ref], [sides_a, sides_s], [run_a, run_s], wa_ref, hid_a, carry_a, cols_a, own_a, unroll)
    blended_sides(TO_COMMON, turn, own_a, flip, out_a)
    atmos = Exchange(out_a, ha2, False, sem_a.at[0], sem_a.at[1], near.at[1])
    atmos.start()
    load_o.wait()
    wait_back()
    first, last = lanes(CS) == 0, lanes(CS) == S - 1

    def put(i, _):
        for u in range(4):
            b = i * 4 + u
            v = got[slot_ref[b]]
            force[b] = v
            cols_f[0] = roll(jnp.where(first, v, cols_f[0]), -1)
            cols_f[1] = jnp.where(last, v, roll(cols_f[1], -1))
        return 0

    lax.fori_loop(0, S // 4, put, 0)
    own_f[UP], own_f[DOWN], own_f[LEFT], own_f[RIGHT] = force[0], force[S - 1], cols_f[0], cols_f[1]
    forcing = Exchange(own_f, hf, True, sem_f.at[0], sem_f.at[1], near.at[2])
    forcing.start()
    forcing.wait()
    folded_sides(hf, sides_f)
    hidden_rows([x_o, force], [sides_o, sides_f], [run_o, run_f], wo_ref, hid_o, carry_o, cols_o, own_o, unroll)
    ocean = Exchange(own_o, ho2, True, sem_o.at[0], sem_o.at[1], near.at[2])
    ocean.start()
    atmos.wait()
    ocean.wait()


def second_exchange(slots, turn, back, es, xa, xo, sea, ha, ho, wa, wo, unroll):
    hbm, vm, sm = (pl.BlockSpec(memory_space=m) for m in (pl.ANY, VMEM, SMEM))
    shape = jax.ShapeDtypeStruct
    ca, co = xa.shape[1], xo.shape[1]
    bf = lambda *dims: VMEM(dims, BF)
    return pl.pallas_call(
        partial(second_kernel, unroll),
        out_shape=(
            shape((S, ca, S), BF),
            shape((S, co, S), BF),
            shape((8, ca, S), BF),
            shape((8, co, S), BF),
        ),
        in_specs=[sm, sm] + [hbm] * 4 + [vm] * 5,
        out_specs=(vm, vm, hbm, hbm),
        scratch_shapes=[bf(S, ca, S), bf(S, co, S), bf(8, CS, S), bf(8, CS, S), bf(2 * S, CS, S), bf(S, CS, S)]
        + [bf(8, ca, S), bf(8, CS, S)]
        + [bf(8, ca, S), bf(8, CS, S), bf(8, co, S), bf(8, CS, S)]
        + [bf(4, ca, S), bf(4, CS, S), bf(4, co, S), bf(4, CS, S)]
        + [VMEM((2, ca, 2 * S), F32), VMEM((2, co, 2 * S), F32)]
        + [bf(4, ca, S), bf(4, co, S), bf(2, CS, S)]
        + [bf(4, ca, S), bf(4, ca, S), bf(4, co, S), bf(4, CS, S)]
        + [DMA((2,)), DMA((2,))]
        + [DMA((2, 8))] * 4
        + [DMA((3,))],
        compiler_params=pltpu.CompilerParams(collective_id=1, has_side_effects=True),
        name="second_exchange",
    )(slots, turn, back, es, xa, xo, sea, ha, ho, wa, wo)


def taps(weight):
    _, outs, channels = weight.shape
    return weight.reshape(3, 3, outs, channels).transpose(0, 2, 1, 3).reshape(3 * outs, 3 * channels)


TURNED_TAPS = (
    (0, 1, 2, 3, 4, 5, 6, 7, 8),
    (2, 5, 8, 1, 4, 7, 0, 3, 6),
    (8, 7, 6, 5, 4, 3, 2, 1, 0),
    (6, 3, 0, 7, 4, 1, 8, 5, 2),
)


def on_device(
    atmos_state, ocean_state, land_mask, face_turns, block_target, block_patch, block_weight,
    atmos_w1, atmos_w2, ocean_w1, ocean_w2,
):
    turn = face_turns.reshape(1)
    face = lax.axis_index("face")
    edge = jnp.where(face == 0, 1, jnp.where(face == lax.axis_size("face") - 1, 2, 0))
    edge = edge.astype(jnp.int32).reshape(1)
    mask = jnp.repeat(land_mask, 32, axis=1).astype(BF)
    order = jnp.array(TURNED_TAPS, jnp.int32)[turn[0]]
    wa1 = taps(jnp.take(atmos_w1, order, axis=0))
    wa2 = taps(jnp.take(atmos_w2, order, axis=0))
    wo1, wo2 = taps(ocean_w1), taps(ocean_w2)
    weight = lax.reduce_precision(block_weight[:, 0], 8, 7)
    pay, meta, common, slots = prepare(
        turn, block_target[:, 0], block_patch[:, 0], weight, atmos_state, ocean_state, mask
    )
    pay_in, meta_in, xa, xo, ha, ho = first_exchange(turn, mask, pay, meta, atmos_state, ocean_state)
    sea, es, back = remap(turn, meta_in, pay_in, common)
    hid_a, hid_o, ha2, ho2 = second_exchange(
        slots, turn, back, es.astype(BF), xa, xo, sea, ha, ho, wa1, wo1, 16
    )
    atmos_out = out_conv(False, turn, hid_a, ha2, wa2, atmos_state, mask, 8)
    ocean_out = out_conv(True, edge, hid_o, ho2, wo2, ocean_state, mask, 8)
    return atmos_out, ocean_out


def solution(mesh):
    placed = (
        P(None, "face", "tile"),
        P(None, "face", "tile"),
        P("face", "tile"),
        P("face", "tile"),
        P(("face", "tile"), None),
        P(("face", "tile"), None),
        P(("face", "tile"), None),
        P(),
        P(),
        P(),
        P(),
    )
    return jax.shard_map(
        on_device,
        mesh=mesh,
        in_specs=placed,
        out_specs=(P(None, "face", "tile"), P(None, "face", "tile")),
        check_vma=False,
    )
```

```python
from functools import partial

import jax
import jax.numpy as jnp
from jax import lax
from jax.experimental import pallas as pl
from jax.experimental.pallas import tpu as pltpu
from jax.sharding import PartitionSpec as P

BF = jnp.bfloat16
F32 = jnp.float32
S = 128
CS = 16
MESH = pl.DeviceIdType.MESH
DMA = pltpu.SemaphoreType.DMA
VMEM = pltpu.VMEM
SMEM = pltpu.SMEM

UP, DOWN, LEFT, RIGHT, UL, UR, DL, DR = range(8)
TO_STORED = (
    ((UP, 0), (RIGHT, 0), (DOWN, 1), (LEFT, 1)),
    ((DOWN, 0), (LEFT, 0), (UP, 1), (RIGHT, 1)),
    ((LEFT, 0), (UP, 1), (RIGHT, 1), (DOWN, 0)),
    ((RIGHT, 0), (DOWN, 1), (LEFT, 1), (UP, 0)),
    ((UL, 0), (UR, 1), (DR, 1), (DL, 0)),
    ((UR, 0), (DR, 0), (DL, 1), (UL, 1)),
    ((DL, 0), (UL, 0), (UR, 1), (DR, 1)),
    ((DR, 0), (DL, 1), (UL, 1), (UR, 0)),
)
TO_COMMON = (
    ((UP, 0), (LEFT, 1), (DOWN, 1), (RIGHT, 0)),
    ((DOWN, 0), (RIGHT, 1), (UP, 1), (LEFT, 0)),
    ((LEFT, 0), (DOWN, 0), (RIGHT, 1), (UP, 1)),
    ((RIGHT, 0), (UP, 0), (LEFT, 1), (DOWN, 1)),
)


def anti():
    rows = lax.broadcasted_iota(jnp.int32, (S, S), 0)
    cols = lax.broadcasted_iota(jnp.int32, (S, S), 1)
    return jnp.where(rows + cols == S - 1, 1.0, 0.0).astype(BF)


def eye():
    rows = lax.broadcasted_iota(jnp.int32, (S, S), 0)
    cols = lax.broadcasted_iota(jnp.int32, (S, S), 1)
    return jnp.where(rows == cols, 1.0, 0.0).astype(BF)


def dot(a, b):
    return jnp.dot(a, b, preferred_element_type=F32)


def dot_nt(a, b):
    return lax.dot_general(a, b, (((1,), (1,)), ((), ())), preferred_element_type=F32)


def roll(v, shift):
    return pltpu.roll(v, shift % S, 1)


def lanes(channels):
    return lax.broadcasted_iota(jnp.int32, (channels, S), 1)


def reversed_lanes(v):
    return dot(v, anti()).astype(BF)


def select_sides(table, mode, source, target):
    for turn in range(4):

        @pl.when(mode == turn)
        def _():
            for i, row in enumerate(table):
                side, flip = row[turn]
                v = source[side]
                target[i] = reversed_lanes(v) if flip else v


def ocean_sides(mode, source, target):
    for i in range(8):
        target[i] = source[i]

    @pl.when(mode == 1)
    def _():
        for i in (UP, UL, UR):
            target[i] = jnp.zeros_like(target[i])

    @pl.when(mode == 2)
    def _():
        for i in (DOWN, DL, DR):
            target[i] = reversed_lanes(source[i])


def blended_sides(table, mode, source, flipped, target):
    count, channels = source.shape[0], source.shape[1]
    flat = source[...].reshape(count * channels, S)
    flipped[:count] = reversed_lanes(flat).reshape(count, channels, S)
    for i, row in enumerate(table):
        v = None
        for turn, (side, flip) in enumerate(row):
            each = flipped[side] if flip else source[side]
            v = each if v is None else jnp.where(mode == turn, each, v)
        target[i] = v


def folded_sides(source, target):
    f, n_face = lax.axis_index("face"), lax.axis_size("face")
    target[LEFT], target[RIGHT] = source[LEFT], source[RIGHT]
    for i in (UP, UL, UR):

        @pl.when(f == 0)
        def _():
            target[i] = jnp.zeros(target.shape[1:], BF)

        @pl.when(f > 0)
        def _():
            target[i] = source[i]

    for i in (DOWN, DL, DR):

        @pl.when(f == n_face - 1)
        def _():
            target[i] = reversed_lanes(source[i])

        @pl.when(f < n_face - 1)
        def _():
            target[i] = source[i]


def turn_matrix(v, turns):
    if turns == 1:
        return dot_nt(anti(), v)
    if turns == 2:
        return dot(dot(anti(), v).astype(BF), anti())
    if turns == 3:
        return dot_nt(eye(), dot(anti(), v).astype(BF))
    return v.astype(F32)


def conv_rows(parts, sides, runs, w_ref, outs, carry, finish, flush, unroll):
    first = [lanes(p.shape[1]) == 0 for p in parts]
    last = [lanes(p.shape[1]) == S - 1 for p in parts]
    for side, run in zip(sides, runs):
        run[0] = side[LEFT]
        run[1] = roll(side[LEFT], 64)
        run[2] = roll(side[RIGHT], 1)
        run[3] = roll(side[RIGHT], 65)

    def products(r, first_row, end):
        left, centre, right = [], [], []
        for n, (p, side, run) in enumerate(zip(parts, sides, runs)):
            la, lb, ra, rb = run[0], run[1], run[2], run[3]
            run[0], run[1], run[2], run[3] = roll(la, -1), roll(lb, -1), roll(ra, -1), roll(rb, -1)
            if first_row:
                xa, la, ra = side[UP], side[UL], side[UR]
            else:
                xa = p[r - 1]
            if end is None:
                xb = p[r + 63]
            else:
                xb = jnp.where(end, side[DOWN], p[jnp.minimum(r + 63, S - 1)])
                lb, rb = jnp.where(end, side[DL], lb), jnp.where(end, side[DR], rb)
            both = lambda a, b: jnp.concatenate([a, b], axis=1)
            left.append(both(roll(jnp.where(last[n], la, xa), 1), roll(jnp.where(last[n], lb, xb), 1)))
            centre.append(both(xa, xb))
            right.append(both(roll(jnp.where(first[n], ra, xa), -1), roll(jnp.where(first[n], rb, xb), -1)))
        return dot(w_ref[...], jnp.concatenate(left + centre + right, axis=0))

    o = outs
    p0 = products(0, True, None)
    p1 = products(1, False, None)
    carry[0] = p0[:o] + p1[o : 2 * o]
    carry[1] = p1[:o]

    def sixteen(g, _):
        def body(i, _):
            done, near = carry[0], carry[1]
            for u in range(unroll):
                y = g * 16 + i * unroll + u
                p = products(y + 2, False, y == 63 if u == unroll - 1 else None)
                finish(y, done + p[2 * o :])
                done, near = near + p[o : 2 * o], p[:o]
            carry[0], carry[1] = done, near
            return 0

        lax.fori_loop(0, 16 // unroll, body, 0)
        if flush is not None:
            flush(g)
        return 0

    lax.fori_loop(0, 4, sixteen, 0)


def fed_rows(parts, sides, runs, w_ref, outs, carry, feed, held, finish, flush, unroll):
    first = [lanes(p.shape[1]) == 0 for p in parts]
    last = [lanes(p.shape[1]) == S - 1 for p in parts]
    total = sum(p.shape[1] for p in parts)
    for side, run in zip(sides, runs):
        run[0] = side[LEFT]
        run[1] = roll(side[LEFT], 64)
        run[2] = roll(side[RIGHT], 1)
        run[3] = roll(side[RIGHT], 65)

    def build(r, first_row, end, slot):
        at = 0
        for n, (p, side, run) in enumerate(zip(parts, sides, runs)):
            la, lb, ra, rb = run[0], run[1], run[2], run[3]
            run[0], run[1], run[2], run[3] = roll(la, -1), roll(lb, -1), roll(ra, -1), roll(rb, -1)
            if first_row:
                xa, la, ra = side[UP], side[UL], side[UR]
            else:
                xa = p[jnp.minimum(r - 1, S - 1)] if end is not None else p[r - 1]
            if end is None:
                xb = p[r + 63]
            else:
                xb = jnp.where(end, side[DOWN], p[jnp.minimum(r + 63, S - 1)])
                lb, rb = jnp.where(end, side[DL], lb), jnp.where(end, side[DR], rb)
            size = p.shape[1]
            for half, (x, l, r_) in enumerate(((xa, la, ra), (xb, lb, rb))):
                cols = slice(half * S, (half + 1) * S)
                feed[slot, at : at + size, cols] = roll(jnp.where(last[n], l, x), 1)
                feed[slot, total + at : total + at + size, cols] = x
                feed[slot, 2 * total + at : 2 * total + at + size, cols] = roll(jnp.where(first[n], r_, x), -1)
            at += size

    o = outs
    build(0, True, None, 0)
    build(1, False, None, 1)
    p0 = dot(w_ref[...], feed[0])
    build(2, False, None, 0)
    p1 = dot(w_ref[...], feed[1])
    carry[0] = p0[:o] + p1[o : 2 * o]
    carry[1] = p1[:o]
    if held is not None:
        held[...] = jnp.zeros_like(held)

    def sixteen(g, _):
        def body(i, _):
            done, near = carry[0], carry[1]
            before = None if held is None else held[...]
            for u in range(unroll):
                y = g * 16 + i * unroll + u
                p = dot(w_ref[...], feed[u % 2])
                build(y + 3, False, y >= 62 if u >= unroll - 2 else None, (u + 1) % 2)
                if held is not None or u:
                    finish(y - 1, before)
                before = done + p[2 * o :]
                done, near = near + p[o : 2 * o], p[:o]
            if held is None:
                finish(y, before)
            else:
                held[...] = before
            carry[0], carry[1] = done, near
            return 0

        lax.fori_loop(0, 16 // unroll, body, 0)
        if flush is not None:
            flush(g)
        return 0

    lax.fori_loop(0, 4, sixteen, 0)
    if held is not None:
        finish(63, held[...])


def hidden_rows(parts, sides, runs, w_ref, hid_ref, carry, cols, own, unroll, feed=None, held=None):
    outs = hid_ref.shape[1]
    first, last = lanes(outs) == 0, lanes(outs) == S - 1
    cols[...] = jnp.zeros_like(cols)

    def finish(y, both):
        for half in range(2):
            v = jax.nn.gelu(both[:, half * S : (half + 1) * S], approximate=True).astype(BF)
            hid_ref[(y if feed is None else jnp.maximum(y, 0)) + 64 * half] = v
            cols[half] = roll(jnp.where(first, v, cols[half]), -1)
            cols[2 + half] = jnp.where(last, v, roll(cols[2 + half], -1))

    if feed is None:
        conv_rows(parts, sides, runs, w_ref, outs, carry, finish, None, unroll)
    else:
        fed_rows(parts, sides, runs, w_ref, outs, carry, feed, held, finish, None, unroll)
    upper = lanes(outs) >= 64
    own[UP], own[DOWN] = hid_ref[0], hid_ref[S - 1]
    own[LEFT] = jnp.where(upper, cols[1], roll(cols[0], 64))
    own[RIGHT] = jnp.where(upper, cols[3], roll(cols[2], 64))


def out_rows(ocean, hid, side, run, w_ref, base, mask_ref, out, target, sem, carry, feed, stage, unroll):
    outs = hid.shape[1]

    def part(g, half):
        rows = pl.ds(pl.multiple_of(g * 16 + 64 * half, 16), 16)
        return pltpu.make_async_copy(out.at[:, rows, :], target.at[:, rows, :], sem.at[g, half])

    def finish(y, both):
        place = lax.rem(y, 16)
        for half in range(2):
            stage[half, pl.ds(place, outs, stride=16), :] = both[:, half * S : (half + 1) * S]

    def flush(g):
        for half in range(2):
            rows = pl.ds(pl.multiple_of(g * 16 + 64 * half, 16), 16)
            kept = base[:, rows, :].astype(F32)
            summed = stage[half].reshape(outs, 16, S)
            if ocean:
                gate = mask_ref[rows, :].astype(F32)[None]
                out[:, rows, :] = (gate * (gate * kept + summed)).astype(BF)
            else:
                out[:, rows, :] = (kept + summed).astype(BF)
            part(g, half).start()

    fed_rows([hid], [side], [run], w_ref, outs, carry, feed, None, finish, flush, unroll)

    def wait():
        for g in range(4):
            for half in range(2):
                part(g, half).wait()

    return wait


def outs_kernel(
    turn_ref, edge_ref, hid_a, hid_o, ha_ref, ho_ref, wa_ref, wo_ref, base_a, base_o, mask_ref, out_a, out_o,
    h_a, h_o, b_a, b_o, o_a, o_o, side_a, side_o, run_a, run_o, carry_a, carry_o, feed_a, feed_o, stage_a, stage_o,
    loads, sem_a, sem_o,
):
    pairs = ((hid_o, h_o), (base_o, b_o), (hid_a, h_a), (base_a, b_a))
    copies = [pltpu.make_async_copy(src, dst, loads.at[n]) for n, (src, dst) in enumerate(pairs)]
    for each in copies:
        each.start()
    ocean_sides(edge_ref[0], ho_ref, side_o)
    select_sides(TO_STORED, turn_ref[0], ha_ref, side_a)
    copies[0].wait()
    copies[1].wait()
    wait_o = out_rows(True, h_o, side_o, run_o, wo_ref, b_o, mask_ref, o_o, out_o, sem_o, carry_o, feed_o, stage_o, 8)
    copies[2].wait()
    copies[3].wait()
    wait_a = out_rows(False, h_a, side_a, run_a, wa_ref, b_a, mask_ref, o_a, out_a, sem_a, carry_a, feed_a, stage_a, 4)
    wait_o()
    wait_a()


def final_convs(turn, edge, hid_a, hid_o, ha, ho, wa, wo, base_a, base_o, mask):
    hbm, vm, sm = (pl.BlockSpec(memory_space=m) for m in (pl.ANY, VMEM, SMEM))
    ca, co = hid_a.shape[1], hid_o.shape[1]
    scratch = []
    for make in (
        lambda c: VMEM((S, c, S), BF),
        lambda c: VMEM((c, S, S), BF),
        lambda c: VMEM((c, S, S), BF),
        lambda c: VMEM((8, c, S), BF),
        lambda c: VMEM((4, c, S), BF),
        lambda c: VMEM((2, c, 2 * S), F32),
        lambda c: VMEM((2, 3 * c, 2 * S), BF),
        lambda c: VMEM((2, c * 16, S), F32),
    ):
        scratch += [make(ca), make(co)]
    return pl.pallas_call(
        outs_kernel,
        out_shape=(jax.ShapeDtypeStruct((ca, S, S), BF), jax.ShapeDtypeStruct((co, S, S), BF)),
        in_specs=[sm, sm, hbm, hbm] + [vm] * 4 + [hbm, hbm, vm],
        out_specs=(hbm, hbm),
        scratch_shapes=scratch + [DMA((4,)), DMA((4, 2)), DMA((4, 2))],
        name="final_convs",
    )(turn, edge, hid_a, hid_o, ha, ho, wa, wo, base_a, base_o, mask)


def prep_kernel(
    turn_ref, target_ref, patch_ref, weight_ref, atmos_ref, ocean_ref, mask_ref,
    pay_ref, meta_ref, common_ref, slot_ref, surf, tally,
):
    turn = turn_ref[0]
    gate = mask_ref[...].astype(F32)[None]
    surf[...] = jnp.swapaxes((ocean_ref[...].astype(F32) * gate).astype(BF), 0, 1)
    pay_ref[...] = jnp.zeros_like(pay_ref)
    meta_ref[...] = jnp.zeros_like(meta_ref)

    def clear(i, _):
        for u in range(8):
            tally[i * 8 + u] = 0
        return 0

    lax.fori_loop(0, S // 8, clear, 0)
    lane = lanes(1)

    def place(i, _):
        for u in range(4):
            b = i * 4 + u
            goal = target_ref[b]
            seen = tally[goal]
            slot = 2 * goal + seen
            tally[goal] = seen + 1
            slot_ref[b] = slot
            pay_ref[slot] = surf[b]
            spot = jnp.full((1, S), patch_ref[b], jnp.int32).astype(F32)
            meta_ref[slot] = jnp.where(lane == 0, spot, weight_ref[b])
        return 0

    lax.fori_loop(0, S // 4, place, 0)
    for quarter in range(4):

        @pl.when(turn == quarter)
        def _():
            for c in range(CS):
                common_ref[c] = turn_matrix(atmos_ref[c], (4 - quarter) % 4).astype(BF)


def prepare(turn, target, patch, weight, atmos, ocean, mask):
    sm = pl.BlockSpec(memory_space=SMEM)
    head = pl.BlockSpec((CS, S, S), lambda i: (0, 0, 0))
    whole = lambda shape: pl.BlockSpec(shape, lambda i: (0,) * len(shape))
    shape = jax.ShapeDtypeStruct
    return pl.pallas_call(
        prep_kernel,
        grid=(1,),
        out_shape=(
            shape((2 * S, CS, S), BF),
            shape((2 * S, 1, S), F32),
            shape((CS, S, S), BF),
            shape((S,), jnp.int32),
        ),
        in_specs=[sm] * 4 + [head, head, whole((S, S))],
        out_specs=(whole((2 * S, CS, S)), whole((2 * S, 1, S)), whole((CS, S, S)), sm),
        scratch_shapes=[VMEM((S, CS, S), BF), SMEM((S,), jnp.int32)],
        name="prepare",
    )(turn, target, patch, weight, atmos, ocean, mask)


def remap_blocks(turn, meta_ref, in_ref, common_ref, sea_ref, side_ref, back_ref, wide, total, spread, edges):
    high, odd = turn >= 2, (turn % 2) == 1
    meta = meta_ref[...].reshape(2 * S, S)
    spot = jnp.broadcast_to(meta[:, 0:1], (2 * S, S))
    share = jnp.broadcast_to(meta[:, 1:2], (2 * S, S))
    row = lax.broadcasted_iota(jnp.int32, (2 * S, S), 1)
    pick = jnp.where(spot == row.astype(F32), 1.0, 0.0).astype(BF)
    faces = spot == jnp.where(high, S - 1 - row, row).astype(F32)
    spread[...] = dot_nt(eye(), jnp.where(faces, share, 0.0).astype(BF)).astype(BF)
    amount = jnp.maximum(dot(spread[...], jnp.ones((2 * S, S), BF)), 1.0)
    wide[...] = in_ref[...].astype(F32).reshape(wide.shape)
    sides = lax.broadcasted_iota(jnp.int32, (16, S), 0)
    along = lax.broadcasted_iota(jnp.int32, (16, S), 1)
    ends = jnp.where(along == jnp.where(sides < 2, sides * (S - 1), -1), 1.0, 0.0).astype(BF)
    plain, turned = eye().astype(F32), anti().astype(F32)
    upright = jnp.where(high, turned, plain).astype(BF)
    after = jnp.where(turn == 2, turned, plain).astype(BF)
    ahead = jnp.where(turn == 1, turned, plain).astype(BF)
    for c in range(CS):
        strip = pl.ds(c, 2 * S, stride=CS)
        blocks = wide[strip, :].astype(BF)
        v = (dot(spread[...], blocks) / amount).astype(BF)
        wide[strip, :] = dot(pick, common_ref[c])
        total[pl.ds(c, S, stride=CS), :] = jnp.where(odd, dot_nt(ahead, v), dot(v, after))
        edge = dot(dot_nt(ends, v).astype(BF), upright)
        low_row, high_row = v.astype(F32)[0:1], v.astype(F32)[S - 1 : S]
        edges[UP, pl.ds(c, 1), :] = jnp.where(high, high_row, low_row)
        edges[DOWN, pl.ds(c, 1), :] = jnp.where(high, low_row, high_row)
        edges[LEFT, pl.ds(c, 1), :] = edge[0:1]
        edges[RIGHT, pl.ds(c, 1), :] = edge[1:2]
    side_ref[...] = edges[...].astype(BF)
    back_ref[...] = wide[...].reshape(2 * S, CS, S).astype(BF)
    sea_ref[...] = total[...].reshape(S, CS, S).astype(BF)


class Exchange:
    def __init__(self, src, dst, ocean, send, recv, near):
        f, t = lax.axis_index("face"), lax.axis_index("tile")
        n_face, n_tile = lax.axis_size("face"), lax.axis_size("tile")
        fu, fd = (f + n_face - 1) % n_face, (f + 1) % n_face
        tl, tr = (t + n_tile - 1) % n_tile, (t + 1) % n_tile
        copy = lambda n, side, slot, device: pltpu.make_async_remote_copy(
            src_ref=src.at[side],
            dst_ref=dst.at[slot],
            send_sem=send.at[n],
            recv_sem=recv.at[slot],
            device_id=device,
            device_id_type=MESH,
        )
        always, top, bottom = None, f > 0, f < n_face - 1
        if not ocean:
            top = bottom = None
        self.copies = [
            (always, copy(0, LEFT, RIGHT, (f, tl))),
            (always, copy(1, RIGHT, LEFT, (f, tr))),
            (top, copy(2, UP, DOWN, (fu, t))),
            (top, copy(3, UP, DR, (fu, tl))),
            (top, copy(4, UP, DL, (fu, tr))),
            (bottom, copy(5, DOWN, UP, (fd, t))),
            (bottom, copy(6, DOWN, UR, (fd, tl))),
            (bottom, copy(7, DOWN, UL, (fd, tr))),
        ]
        self.local = []
        self.arrivals = [(None, LEFT), (None, RIGHT)]
        if ocean:
            fold = f == n_face - 1
            inner = fold & (lax.rem(t, n_tile // 2) != 0)
            outer = fold & (lax.rem(t, n_tile // 2) != n_tile // 2 - 1)
            left_to, right_to = (2 * n_tile - t) % n_tile, (2 * n_tile - 2 - t) % n_tile
            self.copies += [
                (fold, copy(5, DOWN, DOWN, (f, n_tile - 1 - t))),
                (inner, copy(6, DOWN, DL, (f, left_to))),
                (outer, copy(7, DOWN, DR, (f, right_to))),
            ]
            own_left = fold & (lax.rem(t, n_tile // 2) == 0)
            own_right = fold & (lax.rem(t, n_tile // 2) == n_tile // 2 - 1)
            self.local = [
                (own_left, pltpu.make_async_copy(src.at[DOWN], dst.at[DL], near)),
                (own_right, pltpu.make_async_copy(src.at[DOWN], dst.at[DR], near)),
            ]
            self.arrivals += [(top, UP), (top, UL), (top, UR), (None, DOWN)]
            self.arrivals += [(bottom | inner, DL), (bottom | outer, DR)]
        else:
            self.arrivals += [(None, n) for n in (UP, DOWN, UL, UR, DL, DR)]
        self.arrived = lambda slot: copy(0, LEFT, slot, (f, tl)).wait_recv()

    @staticmethod
    def given(condition, act):
        if condition is None:
            act()
        else:
            pl.when(condition)(act)

    def start(self):
        for condition, each in self.copies + self.local:
            self.given(condition, each.start)

    def wait(self):
        for condition, slot in self.arrivals:
            self.given(condition, partial(self.arrived, slot))
        for condition, each in self.local:
            self.given(condition, each.wait)
        for condition, each in self.copies:
            self.given(condition, each.wait_send)


def place():
    f, t = lax.axis_index("face"), lax.axis_index("tile")
    n_tile = lax.axis_size("tile")
    return f * n_tile + t, lax.axis_size("face") * n_tile, n_tile


def each_peer(act):
    f, t = lax.axis_index("face"), lax.axis_index("tile")
    n_face, n_tile = lax.axis_size("face"), lax.axis_size("tile")

    def wrapped(at, count):
        return jnp.where(at >= count, at - count, at)

    def one(df, dt):
        act(wrapped(f + df, n_face), wrapped(t + dt, n_tile))
        return 0

    lax.fori_loop(1, n_tile, lambda dt, _: one(0, dt), 0)
    lax.fori_loop(1, n_face, lambda df, _: lax.fori_loop(0, n_tile, lambda dt, _: one(df, dt), 0), 0)


def meet_all():
    me, count, n_tile = place()
    barrier = pltpu.get_barrier_semaphore()
    each_peer(lambda face, tile: pl.semaphore_signal(barrier, inc=1, device_id=(face, tile), device_id_type=MESH))
    pl.semaphore_wait(barrier, count - 1)


def everyone(src, dst, rows, send, recv, near):
    me, count, n_tile = place()

    def send_to(face, tile):
        pltpu.make_async_remote_copy(
            src_ref=src.at[pl.ds((face * n_tile + tile) * rows, rows)],
            dst_ref=dst.at[pl.ds(me * rows, rows)],
            send_sem=send,
            recv_sem=recv,
            device_id=(face, tile),
            device_id_type=MESH,
        ).start()

    own = pltpu.make_async_copy(src.at[pl.ds(me * rows, rows)], dst.at[pl.ds(me * rows, rows)], near)
    other = (lax.axis_index("face"), (lax.axis_index("tile") + 1) % n_tile)
    rest = pltpu.make_async_remote_copy(
        src_ref=src.at[pl.ds(0, (count - 1) * rows)],
        dst_ref=dst.at[pl.ds(0, (count - 1) * rows)],
        send_sem=send,
        recv_sem=recv,
        device_id=other,
        device_id_type=MESH,
    )

    def start():
        each_peer(send_to)
        own.start()

    def wait():
        own.wait()
        rest.wait_recv()
        rest.wait_send()

    return start, wait


def main_kernel(
    slot_ref, turn_ref, mask_ref, common_ref, wa_ref, wo_ref, pay, meta, atmos, ocean,
    hid_a_out, hid_o_out, ha2, ho2,
    held_a, held_o, x_a, x_o, hid_a, hid_o, wide_a, wide_o, pay_in, meta_in, back, got, force, sea,
    wide_s, total, spread, edges, ha, ho, hs, hf, side_s, flip, flip_s,
    sides_a, sides_s, sides_o, sides_f, run_a, run_s, run_o, run_f,
    carry_a, carry_o, cols_a, cols_o, cols_f, own_a, own_o, own_f, out_a, out_o, feed, held,
    loads, sem_m, sem_p, sem_b, sem_xa, sem_xo, sem_s, sem_f, sem_a, sem_o, near, saves,
):
    turn = turn_ref[0]

    def load(g, n):
        source, kept = ((atmos, held_a), (ocean, held_o))[n]
        rows = pl.ds(pl.multiple_of(g * 16, 16), 16)
        return pltpu.make_async_copy(source.at[:, rows, :], kept.at[g], loads.at[n, g])

    for g in range(8):
        for n in range(2):
            load(g, n).start()
    meet_all()
    start_meta, wait_meta = everyone(meta, meta_in, 2, sem_m.at[0], sem_m.at[1], near.at[0])
    start_pay, wait_pay = everyone(pay, pay_in, 2, sem_p.at[0], sem_p.at[1], near.at[1])
    start_meta()
    start_pay()

    def columns(cols, v):
        first, last = lanes(v.shape[0]) == 0, lanes(v.shape[0]) == S - 1
        cols[0] = roll(jnp.where(first, v, cols[0]), -1)
        cols[1] = jnp.where(last, v, roll(cols[1], -1))

    def sixteen(g, _):
        for n in range(2):
            load(g, n).wait()
        rows = pl.ds(pl.multiple_of(g * 16, 16), 16)
        wide_a[...] = held_a[g].astype(F32).reshape(wide_a.shape)
        gate = mask_ref[rows, :].astype(F32)[None]
        wide_o[...] = (held_o[g].astype(F32) * gate).reshape(wide_o.shape)
        for y in range(16):
            v = wide_a[pl.ds(y, wide_a.shape[0] // 16, stride=16), :].astype(BF)
            x_a[g * 16 + y] = v
            columns(cols_a, v)
            v = wide_o[pl.ds(y, wide_o.shape[0] // 16, stride=16), :].astype(BF)
            x_o[g * 16 + y] = v
            columns(cols_o, v)
        return 0

    cols_a[...] = jnp.zeros_like(cols_a)
    cols_o[...] = jnp.zeros_like(cols_o)
    cols_f[...] = jnp.zeros_like(cols_f)
    lax.fori_loop(0, 8, sixteen, 0)
    own_a[UP], own_a[DOWN], own_a[LEFT], own_a[RIGHT] = x_a[0], x_a[S - 1], cols_a[0], cols_a[1]
    own_o[UP], own_o[DOWN], own_o[LEFT], own_o[RIGHT] = x_o[0], x_o[S - 1], cols_o[0], cols_o[1]
    blended_sides(TO_COMMON, turn, own_a, flip, out_a.at[0])
    state = Exchange(out_a.at[0], ha, False, sem_xa.at[0], sem_xa.at[1], near.at[2])
    masked = Exchange(own_o, ho, True, sem_xo.at[0], sem_xo.at[1], near.at[2])
    state.start()
    masked.start()
    wait_meta()
    wait_pay()
    remap_blocks(turn, meta_in, pay_in, common_ref, sea, side_s, back, wide_s, total, spread, edges)
    start_back, wait_back = everyone(back, got, 2, sem_b.at[0], sem_b.at[1], near.at[0])
    surface = Exchange(side_s, hs, False, sem_s.at[0], sem_s.at[1], near.at[1])
    surface.start()
    start_back()
    state.wait()
    masked.wait()
    blended_sides(TO_STORED, turn, ha, flip, sides_a)
    folded_sides(ho, sides_o)
    surface.wait()
    blended_sides(TO_STORED, turn, hs, flip_s, sides_s)
    hidden_rows([x_a, sea], [sides_a, sides_s], [run_a, run_s], wa_ref, hid_a, carry_a, cols_a, own_a, 2, feed, held)
    save_a = pltpu.make_async_copy(hid_a, hid_a_out, saves.at[0])
    save_a.start()
    blended_sides(TO_COMMON, turn, own_a, flip, out_a.at[1])
    around_a = Exchange(out_a.at[1], ha2, False, sem_a.at[0], sem_a.at[1], near.at[1])
    around_a.start()
    wait_back()
    first, last = lanes(CS) == 0, lanes(CS) == S - 1

    def put(i, _):
        for u in range(8):
            b = i * 8 + u
            v = got[slot_ref[b]]
            force[b] = v
            cols_f[0] = roll(jnp.where(first, v, cols_f[0]), -1)
            cols_f[1] = jnp.where(last, v, roll(cols_f[1], -1))
        return 0

    lax.fori_loop(0, S // 8, put, 0)
    own_f[UP], own_f[DOWN], own_f[LEFT], own_f[RIGHT] = force[0], force[S - 1], cols_f[0], cols_f[1]
    forcing = Exchange(own_f, hf, True, sem_f.at[0], sem_f.at[1], near.at[2])
    forcing.start()
    forcing.wait()
    folded_sides(hf, sides_f)
    hidden_rows([x_o, force], [sides_o, sides_f], [run_o, run_f], wo_ref, hid_o, carry_o, cols_o, out_o, 16)
    around_o = Exchange(out_o, ho2, True, sem_o.at[0], sem_o.at[1], near.at[2])
    around_o.start()
    save_o = pltpu.make_async_copy(hid_o, hid_o_out, saves.at[1])
    save_o.start()
    around_a.wait()
    around_o.wait()
    save_a.wait()
    save_o.wait()


def main(slots, turn, mask, common, wa, wo, pay, meta, atmos, ocean):
    hbm, vm, sm = (pl.BlockSpec(memory_space=m) for m in (pl.ANY, VMEM, SMEM))
    shape = jax.ShapeDtypeStruct
    ca, co = atmos.shape[0], ocean.shape[0]
    bf = lambda *dims: VMEM(dims, BF)
    fl = lambda *dims: VMEM(dims, F32)
    return pl.pallas_call(
        main_kernel,
        out_shape=(
            shape((S, ca, S), BF),
            shape((S, co, S), BF),
            shape((8, ca, S), BF),
            shape((8, co, S), BF),
        ),
        in_specs=[sm, sm] + [vm] * 4 + [hbm] * 4,
        out_specs=(hbm,) * 4,
        scratch_shapes=[bf(8, ca, 16, S), bf(8, co, 16, S), bf(S, ca, S), bf(S, co, S), bf(S, ca, S), bf(S, co, S)]
        + [fl(ca * 16, S), fl(co * 16, S), bf(2 * S, CS, S), fl(2 * S, 1, S)]
        + [bf(2 * S, CS, S), bf(2 * S, CS, S), bf(S, CS, S), bf(S, CS, S)]
        + [fl(2 * S * CS, S), fl(S * CS, S), bf(S, 2 * S), fl(4, CS, S)]
        + [bf(8, ca, S), bf(8, co, S), bf(8, CS, S), bf(8, CS, S), bf(4, CS, S), bf(8, ca, S), bf(8, CS, S)]
        + [bf(8, ca, S), bf(8, CS, S), bf(8, co, S), bf(8, CS, S)]
        + [bf(4, ca, S), bf(4, CS, S), bf(4, co, S), bf(4, CS, S)]
        + [fl(2, ca, 2 * S), fl(2, co, 2 * S), bf(4, ca, S), bf(4, co, S), bf(2, CS, S)]
        + [bf(4, ca, S), bf(4, co, S), bf(4, CS, S), bf(2, 4, ca, S), bf(4, co, S)]
        + [bf(2, 3 * (ca + CS), 2 * S), fl(ca, 2 * S)]
        + [DMA((2, 8)), DMA((2,)), DMA((2,)), DMA((2,))]
        + [DMA((2, 8))] * 6
        + [DMA((3,)), DMA((2,))],
        compiler_params=pltpu.CompilerParams(collective_id=0, has_side_effects=True),
        name="main",
    )(slots, turn, mask, common, wa, wo, pay, meta, atmos, ocean)


def taps(weight):
    _, outs, channels = weight.shape
    return weight.reshape(3, 3, outs, channels).transpose(0, 2, 1, 3).reshape(3 * outs, 3 * channels)


TURNED_TAPS = (
    (0, 1, 2, 3, 4, 5, 6, 7, 8),
    (2, 5, 8, 1, 4, 7, 0, 3, 6),
    (8, 7, 6, 5, 4, 3, 2, 1, 0),
    (6, 3, 0, 7, 4, 1, 8, 5, 2),
)


def on_device(
    atmos_state, ocean_state, land_mask, face_turns, block_target, block_patch, block_weight,
    atmos_w1, atmos_w2, ocean_w1, ocean_w2,
):
    turn = face_turns.reshape(1)
    face = lax.axis_index("face")
    edge = jnp.where(face == 0, 1, jnp.where(face == lax.axis_size("face") - 1, 2, 0))
    edge = edge.astype(jnp.int32).reshape(1)
    mask = jnp.repeat(land_mask, 32, axis=1).astype(BF)
    order = jnp.array(TURNED_TAPS, jnp.int32)[turn[0]]
    wa1 = taps(jnp.take(atmos_w1, order, axis=0))
    wa2 = taps(jnp.take(atmos_w2, order, axis=0))
    wo1, wo2 = taps(ocean_w1), taps(ocean_w2)
    weight = lax.reduce_precision(block_weight[:, 0], 8, 7)
    pay, meta, common, slots = prepare(
        turn, block_target[:, 0], block_patch[:, 0], weight, atmos_state, ocean_state, mask
    )
    hid_a, hid_o, ha, ho = main(slots, turn, mask, common, wa1, wo1, pay, meta, atmos_state, ocean_state)
    atmos_out, ocean_out = final_convs(
        turn, edge, hid_a, hid_o, ha, ho, wa2, wo2, atmos_state, ocean_state, mask
    )
    return atmos_out, ocean_out


def solution(mesh):
    placed = (
        P(None, "face", "tile"),
        P(None, "face", "tile"),
        P("face", "tile"),
        P("face", "tile"),
        P(("face", "tile"), None),
        P(("face", "tile"), None),
        P(("face", "tile"), None),
        P(),
        P(),
        P(),
        P(),
    )
    return jax.shard_map(
        on_device,
        mesh=mesh,
        in_specs=placed,
        out_specs=(P(None, "face", "tile"), P(None, "face", "tile")),
        check_vma=False,
    )
```
